512 devices in a mesh: rows: 64 (over x, z_lo, y), feat: 8 (over z_hi, core).
Axes of the slice: x: 4, y: 8, z: 8 (z_hi: 4, z_lo: 2; z = z_hi * 2 + z_lo), core: 2. Of those that a mesh axis runs over, the one named last changes fastest.
Arguments:
- descriptors: bfloat16 [16384, 128], P('rows'), may hold values from -6 to 6
- freqs: bfloat16 [128, 32768], P(None, 'feat'), may hold values from -0.5 to 0.5
- phases: float32 [32768], P('feat'), may hold values from -3.140625 to 3.140625
- row_weight: float32 [16384], P('rows'), may hold values from 0.3 to 15, as said below
- resid: float32 [16384, 128], P('rows'), may hold values from -6 to 6
- coef: float32 [32768, 128], P(('feat', 'rows')), may hold values from -4 to 4
- direction: float32 [32768, 128], P(('feat', 'rows')), may hold values from -6 to 6
- ridge: float32 [128], replicated, may hold values from 1 to 10
- gamma: float32 [128], replicated, may hold values from 300000 to 3000000
Outputs:
- coef_new: float32 [32768, 128], P(('feat', 'rows'))
- resid_new: float32 [16384, 128], P('rows')
- direction_new: float32 [32768, 128], P(('feat', 'rows'))
- gamma_new: float32 [128], replicated
The draws below stay inside these ranges and needn't reach their ends.
Inputs may be any that keep to these rules, and one draw needn't show every extreme that they name: `row_weight`: positive weights of the profile rows.
All inputs are finite; a program needn't handle non-finite values.
Results may differ from the reference program's by a relative error of at most 0.0006.
The reference program's roundings to bfloat16 on the way count: a program that leaves them out, or rounds other values in their place, can miss the bound.
Values may be sent and summed in bfloat16 or wider, within the bound.
No kernel may reach another device: no remote copies, remote signals or barrier semaphores. Data moves between devices by JAX's collectives and lax.ppermute only.
A program may use at most 64 MiB of HBM per device.

```python
import math
import jax
import jax.numpy as jnp
from jax import lax

DESC = 128
TARGETS = 128
FEAT = 32768
ROWS = 16384


def draw_row_weight(key, part):
    ramp = 1.0 + 2.0 * jnp.arange(ROWS, dtype=jnp.float32) / max(ROWS - 1, 1)
    spread = jnp.exp(jax.random.uniform(key, (ROWS,), jnp.float32, 0.0, math.log(10.0)))
    return 0.3 * ramp * spread


def steps_of(own_key, dims, cuts, low, high):
    factor_of = 1.0
    for dim, shards_of in cuts:
        steps = jax.random.uniform(jax.random.fold_in(jax.random.fold_in(own_key, 6), dim), (shards_of,), jnp.float32, low / len(cuts), high / len(cuts))
        factor_of = factor_of * jnp.repeat(jnp.exp(steps), dims[dim] // shards_of).reshape((-1,) + (1,) * (len(dims) - 1 - dim))
    return factor_of


def centred(own_key, dims, scale, limit, split=(), kind=jnp.bfloat16):
    entries = scale * jax.random.normal(own_key, dims, jnp.float32)
    if split:
        entries = entries * steps_of(own_key, dims, split, -0.22, 0.18)
    return jnp.clip(entries, -limit, limit).astype(kind)


def setup_inputs(seed: int = 0) -> dict:
    arg_keys = jax.random.split(jax.random.key(seed), 10)
    return {
        "descriptors": centred(arg_keys[0], (ROWS, DESC), 1.0, 6.0, ((0, 64),)),
        "freqs": centred(arg_keys[1], (DESC, FEAT), DESC ** -0.5, 0.5, ((1, 8),)),
        "phases": jnp.clip(jax.random.uniform(arg_keys[2], (FEAT,), jnp.float32, -3.140625, 3.140625), -3.140625, 3.140625),
        "row_weight": draw_row_weight(jax.random.fold_in(arg_keys[9], 71), 0),
        "resid": centred(arg_keys[4], (ROWS, TARGETS), 1.0, 6.0, ((0, 64),), jnp.float32),
        "coef": centred(arg_keys[5], (FEAT, TARGETS), 0.3, 4.0, ((0, 512),), jnp.float32),
        "direction": centred(arg_keys[6], (FEAT, TARGETS), 1.0, 6.0, ((0, 512),), jnp.float32),
        "ridge": jnp.clip(jnp.exp(jax.random.uniform(arg_keys[7], (TARGETS,), jnp.float32, math.log(1.0), math.log(10.0))), 1.0, 10.0),
        "gamma": jnp.clip(jnp.exp(jax.random.uniform(arg_keys[8], (TARGETS,), jnp.float32, math.log(300000.0), math.log(3000000))), 300000.0, 3000000),
    }


def make_features(block_x, freqs, phases):
    scale = math.sqrt(2.0 / FEAT)
    angle = jnp.dot(block_x, freqs, preferred_element_type=jnp.float32) + phases[None, :]
    return (scale * jnp.cos(angle)).astype(jnp.bfloat16)

def reference(descriptors, freqs, phases, row_weight, resid, coef, direction, ridge, gamma):
    block = min(512, ROWS)
    count = ROWS // block
    stacked = descriptors.reshape(count, block, DESC)
    direction_b = direction.astype(jnp.bfloat16)

    def image_block(block_x):
        return jnp.dot(make_features(block_x, freqs, phases), direction_b, preferred_element_type=jnp.float32)
    summed = lax.map(image_block, stacked).reshape(ROWS, TARGETS)
    image = row_weight[:, None] * summed
    curvature = lax.optimization_barrier(jnp.sum(image * image, axis=0)) + ridge * lax.optimization_barrier(jnp.sum(direction * direction, axis=0))
    alpha = gamma / curvature
    coef_new = coef + alpha[None, :] * direction
    resid_new = resid - alpha[None, :] * image
    weighted_b = (row_weight[:, None] * resid_new).astype(jnp.bfloat16).reshape(count, block, TARGETS)

    def grad_step(total, pair):
        block_x, block_w = pair
        feats = make_features(block_x, freqs, phases)
        term = lax.dot_general(feats, block_w, (((0,), (0,)), ((), ())), preferred_element_type=jnp.float32)
        return (total + term, None)
    start = jnp.zeros((FEAT, TARGETS), jnp.float32)
    summed_grad, unused = lax.scan(grad_step, start, (stacked, weighted_b))
    gradient = summed_grad - ridge[None, :] * coef_new
    gamma_new = lax.optimization_barrier(jnp.sum(gradient * gradient, axis=0))
    direction_new = gradient + (gamma_new / gamma)[None, :] * direction
    return (coef_new, resid_new, direction_new, gamma_new)
```

```python
import jax
import jax.numpy as jnp
import numpy as np
from jax import lax
from jax.sharding import Mesh, PartitionSpec as P

AXES = ("x", "zl", "y", "zh", "core")
SIZES = (4, 2, 8, 4, 2)
ROWS = ("x", "zl", "y")
FEAT = ("zh", "core")
PLANE = ("x", "y")
COLUMN = ("zl", "zh", "core")

SCALE = 2.0**-7
TURN = 1.0 / (2.0 * np.pi)
TURN_HI = 6.28125
TURN_LO = 2.0 * np.pi - 6.28125
COS = (
    1.0,
    -0.49999988079071045,
    0.041666485369205475,
    -0.0013887786772102118,
    2.476951885910239e-05,
    -2.707541852942086e-07,
    1.7231808202566867e-09,
)


def scaled_cos(angle):
    turns = jnp.round(angle * jnp.float32(TURN))
    rest = (angle - turns * jnp.float32(TURN_HI)) - turns * jnp.float32(TURN_LO)
    square = rest * rest
    value = jnp.float32(COS[-1] * SCALE)
    for c in COS[-2::-1]:
        value = value * square + jnp.float32(c * SCALE)
    return value


def spread(value, axes):
    n = lax.axis_size(axes)
    copies = jnp.broadcast_to(value[None], (n,) + value.shape)
    return lax.all_to_all(copies, axes, 0, 0, tiled=True)


def total_of(row, axes):
    return jnp.sum(spread(row, axes), axis=0)


def body(descriptors, freqs, phases, row_weight, resid, coef, direction, ridge, gamma):
    rows_dev, desc = descriptors.shape
    targets = resid.shape[1]
    own = direction.shape[0]
    zl = lax.axis_index("zl")
    swap = [(0, 1), (1, 0)]
    n_plane, n_column = lax.axis_size(PLANE), lax.axis_size(COLUMN)

    def both(mine, peer):
        return jnp.where(zl == 0, jnp.concatenate([mine, peer]), jnp.concatenate([peer, mine]))

    rows_x = both(descriptors, lax.ppermute(descriptors, "zl", swap))
    packed = jnp.concatenate([resid, row_weight.reshape(-1, targets)])
    peer = lax.ppermute(packed, "zl", swap)
    rows_resid = both(resid, peer[:rows_dev])
    rows_weight = both(row_weight, peer[rows_dev:].reshape(-1))

    n_x = lax.axis_size("x")
    freq_cols = freqs.reshape(desc, n_x, 2, -1)
    freq_cols = lax.dynamic_index_in_dim(freq_cols, zl, 2, keepdims=False).reshape(desc, -1)
    phase_cols = lax.dynamic_index_in_dim(phases.reshape(n_x, 2, -1), zl, 1, keepdims=False).reshape(-1)

    gathered = spread(direction.astype(jnp.bfloat16), PLANE).reshape(-1, targets)
    angle = jnp.dot(rows_x, freq_cols, preferred_element_type=jnp.float32) + phase_cols[None, :]
    feats = scaled_cos(angle).astype(jnp.bfloat16)
    partial = jnp.dot(feats, gathered, preferred_element_type=jnp.float32)

    penalty = ridge * jnp.sum(direction * direction, axis=0)
    extra = jnp.broadcast_to(penalty[None, None], (n_column, 8, targets))
    sent = jnp.concatenate([partial.reshape(n_column, -1, targets), extra], axis=1)
    came = jnp.sum(lax.all_to_all(sent, COLUMN, 0, 0, tiled=True), axis=0)
    share = came.shape[0] - 8
    image = rows_weight[:, None] * spread(came[:share], COLUMN).reshape(-1, targets)
    curvature = total_of(jnp.sum(image * image, axis=0)[None] + came[share : share + 1], PLANE)
    alpha = gamma / curvature[0]
    coef_new = coef + alpha[None, :] * direction
    rows_new = rows_resid - alpha[None, :] * image
    weighted_b = (rows_weight[:, None] * rows_new).astype(jnp.bfloat16)
    resid_new = lax.dynamic_slice_in_dim(rows_new, zl * rows_dev, rows_dev, 0)

    terms = lax.dot_general(
        feats, weighted_b, (((0,), (0,)), ((), ())), preferred_element_type=jnp.float32
    )
    terms = lax.all_to_all(terms.reshape(n_plane, own, targets), PLANE, 0, 0, tiled=True)
    gradient = jnp.sum(terms, axis=0) - ridge[None, :] * coef_new
    gamma_new = total_of(total_of(jnp.sum(gradient * gradient, axis=0)[None], COLUMN), PLANE)[0]
    direction_new = gradient + (gamma_new / gamma)[None, :] * direction
    return (coef_new, resid_new, direction_new, gamma_new)


def solution(mesh):
    cut = Mesh(mesh.devices.reshape(SIZES), AXES)
    split = P(FEAT + ROWS, None)
    return jax.shard_map(
        body,
        mesh=cut,
        in_specs=(P(ROWS, None), P(None, FEAT), P(FEAT), P(ROWS), P(ROWS, None), split, split, P(), P()),
        out_specs=(split, P(ROWS, None), split, P()),
        check_vma=False,
    )
```

```python
import jax
import jax.numpy as jnp
import numpy as np
from jax import lax
from jax.sharding import Mesh, PartitionSpec as P

AXES = ("x", "zl", "y", "zh", "core")
SIZES = (4, 2, 8, 4, 2)
ROWS = ("x", "zl", "y")
FEAT = ("zh", "core")
PLANE = ("x", "y")
COLUMN = ("zl", "zh", "core")

SCALE = 2.0**-7
TURN = 1.0 / (2.0 * np.pi)
TURN_HI = 6.28125
TURN_LO = 2.0 * np.pi - 6.28125
COS = (
    1.0,
    -0.49999988079071045,
    0.041666485369205475,
    -0.0013887786772102118,
    2.476951885910239e-05,
    -2.707541852942086e-07,
    1.7231808202566867e-09,
)


def scaled_cos(angle):
    turns = jnp.round(angle * jnp.float32(TURN))
    rest = (angle - turns * jnp.float32(TURN_HI)) - turns * jnp.float32(TURN_LO)
    square = rest * rest
    value = jnp.float32(COS[-1] * SCALE)
    for c in COS[-2::-1]:
        value = value * square + jnp.float32(c * SCALE)
    return value


def spread(value, axes):
    n = lax.axis_size(axes)
    copies = jnp.broadcast_to(value[None], (n,) + value.shape)
    return lax.all_to_all(copies, axes, 0, 0, tiled=True)


def total_of(row, axes):
    return jnp.sum(spread(row, axes), axis=0)


def body(descriptors, freqs, phases, row_weight, resid, coef, direction, ridge, gamma):
    rows_dev, desc = descriptors.shape
    targets = resid.shape[1]
    own = direction.shape[0]
    zl = lax.axis_index("zl")
    swap = [(0, 1), (1, 0)]
    n_plane, n_column = lax.axis_size(PLANE), lax.axis_size(COLUMN)

    def both(mine, peer):
        return jnp.where(zl == 0, jnp.concatenate([mine, peer]), jnp.concatenate([peer, mine]))

    copies = jnp.broadcast_to(direction.astype(jnp.bfloat16)[None], (n_plane, own, targets))
    copies, descriptors, resid, row_weight, freqs, phases, direction = lax.optimization_barrier(
        (copies, descriptors, resid, row_weight, freqs, phases, direction)
    )
    gathered = lax.all_to_all(copies, PLANE, 0, 0, tiled=True).reshape(-1, targets)

    rows_x = both(descriptors, lax.ppermute(descriptors, "zl", swap))
    packed = jnp.concatenate([resid, row_weight.reshape(-1, targets)])
    peer = lax.ppermute(packed, "zl", swap)
    rows_resid = both(resid, peer[:rows_dev])
    rows_weight = both(row_weight, peer[rows_dev:].reshape(-1))

    n_x = lax.axis_size("x")
    freq_cols = freqs.reshape(desc, n_x, 2, -1)
    freq_cols = lax.dynamic_index_in_dim(freq_cols, zl, 2, keepdims=False).reshape(desc, -1)
    phase_cols = lax.dynamic_index_in_dim(phases.reshape(n_x, 2, -1), zl, 1, keepdims=False).reshape(-1)
    angle = jnp.dot(rows_x, freq_cols, preferred_element_type=jnp.float32) + phase_cols[None, :]
    feats = scaled_cos(angle).astype(jnp.bfloat16)
    penalty = ridge * jnp.sum(direction * direction, axis=0)
    extra = jnp.broadcast_to(penalty[None, None], (n_column, 8, targets))
    rows_weight = jnp.broadcast_to(rows_weight[:, None], rows_resid.shape)
    first = zl * rows_dev
    gathered, feats, rows_resid, rows_weight, extra, first = lax.optimization_barrier(
        (gathered, feats, rows_resid, rows_weight, extra, first)
    )
    partial = jnp.dot(feats, gathered, preferred_element_type=jnp.float32)

    sent = jnp.concatenate([partial.reshape(n_column, -1, targets), extra], axis=1)
    came = jnp.sum(lax.all_to_all(sent, COLUMN, 0, 0, tiled=True), axis=0)
    share = came.shape[0] - 8
    image = rows_weight * spread(came[:share], COLUMN).reshape(-1, targets)
    curvature = total_of(jnp.sum(image * image, axis=0)[None] + came[share : share + 1], PLANE)
    alpha = gamma / curvature[0]
    coef_new = coef + alpha[None, :] * direction
    rows_new = rows_resid - alpha[None, :] * image
    weighted_b = (rows_weight * rows_new).astype(jnp.bfloat16)
    resid_new = resid - alpha[None, :] * lax.dynamic_slice_in_dim(image, first, rows_dev, 0)
    weighted_b, coef_new, resid_new = lax.optimization_barrier((weighted_b, coef_new, resid_new))

    terms = lax.dot_general(
        feats, weighted_b, (((0,), (0,)), ((), ())), preferred_element_type=jnp.float32
    )
    terms = lax.all_to_all(terms.reshape(n_plane, own, targets), PLANE, 0, 0, tiled=True)
    gradient = jnp.sum(terms, axis=0) - ridge[None, :] * coef_new
    gamma_new = total_of(total_of(jnp.sum(gradient * gradient, axis=0)[None], COLUMN), PLANE)[0]
    direction_new = gradient + (gamma_new / gamma)[None, :] * direction
    return (coef_new, resid_new, direction_new, gamma_new)


def solution(mesh):
    cut = Mesh(mesh.devices.reshape(SIZES), AXES)
    split = P(FEAT + ROWS, None)
    return jax.shard_map(
        body,
        mesh=cut,
        in_specs=(P(ROWS, None), P(None, FEAT), P(FEAT), P(ROWS), P(ROWS, None), split, split, P(), P()),
        out_specs=(split, P(ROWS, None), split, P()),
        check_vma=False,
    )
```

```python
import jax
import jax.numpy as jnp
import numpy as np
from jax import lax
from jax.sharding import Mesh, PartitionSpec as P

AXES = ("x", "zl", "y", "zh", "core")
SIZES = (4, 2, 8, 4, 2)
ROWS = ("x", "zl", "y")
FEAT = ("zh", "core")
PLANE = ("x", "y")
COLUMN = ("zl", "zh", "core")

SCALE = 2.0**-7
TURN = 1.0 / (2.0 * np.pi)
TURN_HI = 6.28125
TURN_LO = 2.0 * np.pi - 6.28125
COS = (
    1.0,
    -0.49999988079071045,
    0.041666485369205475,
    -0.0013887786772102118,
    2.476951885910239e-05,
    -2.707541852942086e-07,
    1.7231808202566867e-09,
)

TERM_MAX = 32000.0
TINY = 1e-30


def scaled_cos(angle):
    turns = jnp.round(angle * jnp.float32(TURN))
    rest = (angle - turns * jnp.float32(TURN_HI)) - turns * jnp.float32(TURN_LO)
    square = rest * rest
    value = jnp.float32(COS[-1] * SCALE)
    for c in COS[-2::-1]:
        value = value * square + jnp.float32(c * SCALE)
    return value


def spread(value, axes):
    n = lax.axis_size(axes)
    copies = jnp.broadcast_to(value[None], (n,) + value.shape)
    return lax.all_to_all(copies, axes, 0, 0, tiled=True)


def total_of(row, axes):
    return jnp.sum(spread(row, axes), axis=0)


def body(descriptors, freqs, phases, row_weight, resid, coef, direction, ridge, gamma):
    rows_dev, desc = descriptors.shape
    targets = resid.shape[1]
    own = direction.shape[0]
    zl = lax.axis_index("zl")
    swap = [(0, 1), (1, 0)]
    n_plane, n_column = lax.axis_size(PLANE), lax.axis_size(COLUMN)

    def both(mine, peer):
        return jnp.where(zl == 0, jnp.concatenate([mine, peer]), jnp.concatenate([peer, mine]))

    copies = jnp.broadcast_to(direction.astype(jnp.bfloat16)[None], (n_plane, own, targets))
    copies, descriptors, resid, row_weight, freqs, phases, direction = lax.optimization_barrier(
        (copies, descriptors, resid, row_weight, freqs, phases, direction)
    )
    gathered = lax.all_to_all(copies, PLANE, 0, 0, tiled=True).reshape(-1, targets)

    rows_x = both(descriptors, lax.ppermute(descriptors, "zl", swap))
    packed = jnp.concatenate([resid, row_weight.reshape(-1, targets)])
    peer = lax.ppermute(packed, "zl", swap)
    rows_resid = both(resid, peer[:rows_dev])
    rows_weight = both(row_weight, peer[rows_dev:].reshape(-1))

    n_x = lax.axis_size("x")
    freq_cols = freqs.reshape(desc, n_x, 2, -1)
    freq_cols = lax.dynamic_index_in_dim(freq_cols, zl, 2, keepdims=False).reshape(desc, -1)
    phase_cols = lax.dynamic_index_in_dim(phases.reshape(n_x, 2, -1), zl, 1, keepdims=False).reshape(-1)
    angle = jnp.dot(rows_x, freq_cols, preferred_element_type=jnp.float32) + phase_cols[None, :]
    feats = scaled_cos(angle).astype(jnp.bfloat16)
    penalty = ridge * jnp.sum(direction * direction, axis=0)
    extra = jnp.broadcast_to(penalty[None, None], (n_column, 8, targets))
    rows_weight = jnp.broadcast_to(rows_weight[:, None], rows_resid.shape)
    resid_size = jnp.sum(jnp.abs(rows_weight * rows_resid), axis=0)
    gathered, feats, rows_resid, rows_weight, extra, resid_size, lower = lax.optimization_barrier(
        (gathered, feats, rows_resid, rows_weight, extra, resid_size, zl == 0)
    )
    partial = jnp.dot(feats, gathered, preferred_element_type=jnp.float32)

    sent = jnp.concatenate([partial.reshape(n_column, -1, targets), extra], axis=1)
    came = jnp.sum(lax.all_to_all(sent, COLUMN, 0, 0, tiled=True), axis=0)
    share = came.shape[0] - 8
    image = rows_weight * spread(came[:share], COLUMN).reshape(-1, targets)
    local = jnp.concatenate([
        jnp.sum(image * image, axis=0)[None] + came[share : share + 1],
        resid_size[None],
        jnp.sum(jnp.abs(rows_weight * image), axis=0)[None],
        jnp.zeros((1, targets), jnp.float32),
    ])
    seen = spread(local, PLANE)
    alpha = gamma / jnp.sum(seen[:, 0], axis=0)
    bound = jnp.max(seen[:, 1], axis=0) + jnp.abs(alpha) * jnp.max(seen[:, 2], axis=0)
    scale = TERM_MAX / jnp.maximum(SCALE * bound, TINY)
    coef_new = coef + alpha[None, :] * direction
    rows_new = rows_resid - alpha[None, :] * image
    weighted_b = (rows_weight * rows_new).astype(jnp.bfloat16)
    resid_new = jnp.where(lower, rows_new[:rows_dev], rows_new[rows_dev:])
    weighted_b, coef_new, resid_new = lax.optimization_barrier((weighted_b, coef_new, resid_new))

    terms = lax.dot_general(
        feats, weighted_b, (((0,), (0,)), ((), ())), preferred_element_type=jnp.float32
    )
    terms = (terms * scale[None, :]).astype(jnp.float16)
    terms = lax.all_to_all(terms.reshape(n_plane, own, targets), PLANE, 0, 0, tiled=True)
    summed = jnp.sum(terms.astype(jnp.float32), axis=0) * (1.0 / scale)[None, :]
    gradient = summed - ridge[None, :] * coef_new
    gamma_new = total_of(total_of(jnp.sum(gradient * gradient, axis=0)[None], COLUMN), PLANE)[0]
    direction_new = gradient + (gamma_new / gamma)[None, :] * direction
    return (coef_new, resid_new, direction_new, gamma_new)


def solution(mesh):
    cut = Mesh(mesh.devices.reshape(SIZES), AXES)
    split = P(FEAT + ROWS, None)
    return jax.shard_map(
        body,
        mesh=cut,
        in_specs=(P(ROWS, None), P(None, FEAT), P(FEAT), P(ROWS), P(ROWS, None), split, split, P(), P()),
        out_specs=(split, P(ROWS, None), split, P()),
        check_vma=False,
    )
```

```python
import jax
import jax.numpy as jnp
import numpy as np
from jax import lax
from jax.experimental import pallas as pl
from jax.sharding import Mesh, PartitionSpec as P

AXES = ("x", "zl", "y", "zh", "core")
SIZES = (4, 2, 8, 4, 2)
ROWS = ("x", "zl", "y")
FEAT = ("zh", "core")
PLANE = ("x", "y")
COLUMN = ("zl", "zh", "core")

SCALE = 2.0**-7
TURN = 1.0 / (2.0 * np.pi)
TURN_HI = 6.28125
TURN_LO = 2.0 * np.pi - 6.28125
COS = (
    1.0,
    -0.49999988079071045,
    0.041666485369205475,
    -0.0013887786772102118,
    2.476951885910239e-05,
    -2.707541852942086e-07,
    1.7231808202566867e-09,
)

TERM_MAX = 32000.0
TINY = 1e-30


def scaled_cos(angle):
    turns = jnp.round(angle * jnp.float32(TURN))
    rest = (angle - turns * jnp.float32(TURN_HI)) - turns * jnp.float32(TURN_LO)
    square = rest * rest
    value = jnp.float32(COS[-1] * SCALE)
    for c in COS[-2::-1]:
        value = value * square + jnp.float32(c * SCALE)
    return value


def rounded_copies(direction_ref, copies_ref):
    rounded = direction_ref[...].astype(copies_ref.dtype)
    copies_ref[...] = jnp.broadcast_to(rounded[None], copies_ref.shape)


def spread(value, axes):
    n = lax.axis_size(axes)
    copies = jnp.broadcast_to(value[None], (n,) + value.shape)
    return lax.all_to_all(copies, axes, 0, 0, tiled=True)


def total_of(row, axes):
    return jnp.sum(spread(row, axes), axis=0)


def body(descriptors, freqs, phases, row_weight, resid, coef, direction, ridge, gamma):
    rows_dev, desc = descriptors.shape
    targets = resid.shape[1]
    own = direction.shape[0]
    zl = lax.axis_index("zl")
    swap = [(0, 1), (1, 0)]
    n_plane, n_column = lax.axis_size(PLANE), lax.axis_size(COLUMN)

    def both(mine, peer):
        return jnp.where(zl == 0, jnp.concatenate([mine, peer]), jnp.concatenate([peer, mine]))

    copies = pl.pallas_call(
        rounded_copies,
        out_shape=jax.ShapeDtypeStruct((n_plane, own, targets), jnp.bfloat16),
        cost_estimate=pl.CostEstimate(flops=0, transcendentals=0, bytes_accessed=4 * own * targets + 2 * n_plane * own * targets),
    )(direction)
    copies, descriptors, resid, row_weight, freqs, phases, direction = lax.optimization_barrier(
        (copies, descriptors, resid, row_weight, freqs, phases, direction)
    )
    gathered = lax.all_to_all(copies, PLANE, 0, 0, tiled=True).reshape(-1, targets)

    rows_x = both(descriptors, lax.ppermute(descriptors, "zl", swap))
    packed = jnp.concatenate([resid, row_weight.reshape(-1, targets)])
    peer = lax.ppermute(packed, "zl", swap)
    rows_resid = both(resid, peer[:rows_dev])
    rows_weight = both(row_weight, peer[rows_dev:].reshape(-1))

    n_x = lax.axis_size("x")
    freq_cols = freqs.reshape(desc, n_x, 2, -1)
    freq_cols = lax.dynamic_index_in_dim(freq_cols, zl, 2, keepdims=False).reshape(desc, -1)
    phase_cols = lax.dynamic_index_in_dim(phases.reshape(n_x, 2, -1), zl, 1, keepdims=False).reshape(-1)
    angle = jnp.dot(rows_x, freq_cols, preferred_element_type=jnp.float32) + phase_cols[None, :]
    feats = scaled_cos(angle).astype(jnp.bfloat16)
    penalty = ridge * jnp.sum(direction * direction, axis=0)
    extra = jnp.broadcast_to(penalty[None, None], (n_column, 8, targets))
    rows_weight = jnp.broadcast_to(rows_weight[:, None], rows_resid.shape)
    resid_size = jnp.sum(jnp.abs(rows_weight * rows_resid), axis=0)
    kind = lax.broadcasted_iota(jnp.int32, (4, targets), 0)
    gathered, feats, rows_resid, rows_weight, extra, resid_size, lower, kind = lax.optimization_barrier(
        (gathered, feats, rows_resid, rows_weight, extra, resid_size, zl == 0, kind)
    )
    partial = jnp.dot(feats, gathered, preferred_element_type=jnp.float32)

    sent = jnp.concatenate([partial.reshape(n_column, -1, targets), extra], axis=1)
    came = jnp.sum(lax.all_to_all(sent, COLUMN, 0, 0, tiled=True), axis=0)
    share = came.shape[0] - 8
    image = rows_weight * spread(came[:share], COLUMN).reshape(-1, targets)
    local = jnp.where(kind == 0, (jnp.sum(image * image, axis=0) + came[share])[None], resid_size[None])
    local = jnp.where(kind == 2, jnp.sum(jnp.abs(rows_weight * image), axis=0)[None], local)
    seen = spread(local, PLANE)
    alpha = gamma / jnp.sum(seen[:, 0], axis=0)
    bound = jnp.max(seen[:, 1], axis=0) + jnp.abs(alpha) * jnp.max(seen[:, 2], axis=0)
    scale = TERM_MAX / jnp.maximum(SCALE * bound, TINY)
    coef_new = coef + alpha[None, :] * direction
    rows_new = rows_resid - alpha[None, :] * image
    weighted_b = (rows_weight * rows_new).astype(jnp.bfloat16)
    resid_new = jnp.where(lower, rows_new[:rows_dev], rows_new[rows_dev:])
    weighted_b, coef_new = lax.optimization_barrier((weighted_b, coef_new))

    terms = lax.dot_general(
        feats, weighted_b, (((0,), (0,)), ((), ())), preferred_element_type=jnp.float32
    )
    terms = (terms * scale[None, :]).astype(jnp.float16)
    terms = lax.all_to_all(terms.reshape(n_plane, own, targets), PLANE, 0, 0, tiled=True)
    terms, resid_new = lax.optimization_barrier((terms, resid_new))
    summed = jnp.sum(terms.astype(jnp.float32), axis=0) * (1.0 / scale)[None, :]
    gradient = summed - ridge[None, :] * coef_new
    gamma_new = total_of(total_of(jnp.sum(gradient * gradient, axis=0)[None], COLUMN), PLANE)[0]
    direction_new = gradient + (gamma_new / gamma)[None, :] * direction
    return (coef_new, resid_new, direction_new, gamma_new)


def solution(mesh):
    cut = Mesh(mesh.devices.reshape(SIZES), AXES)
    split = P(FEAT + ROWS, None)
    return jax.shard_map(
        body,
        mesh=cut,
        in_specs=(P(ROWS, None), P(None, FEAT), P(FEAT), P(ROWS), P(ROWS, None), split, split, P(), P()),
        out_specs=(split, P(ROWS, None), split, P()),
        check_vma=False,
    )
```

```python
import jax
import jax.numpy as jnp
import numpy as np
from jax import lax
from jax.experimental import pallas as pl
from jax.sharding import Mesh, PartitionSpec as P

AXES = ("x", "zl", "y", "zh", "core")
SIZES = (4, 2, 8, 4, 2)
ROWS = ("x", "zl", "y")
FEAT = ("zh", "core")
PLANE = ("x", "y")
COLUMN = ("zl", "zh", "core")
LATE_ZL, LATE_ZH = 1, 2

PLANE_ORDER = [((x + 2) % 4) * 8 + (y + 4) % 8 for x in range(4) for y in range(8)]
COLUMN_ORDER = [((i // 8 + LATE_ZL) % 2) * 8 + ((i // 2 + LATE_ZH) % 4) * 2 + i % 2 for i in range(16)]
ORDERS = {PLANE: PLANE_ORDER, COLUMN: COLUMN_ORDER}

SCALE = 2.0**-7
TURN = 1.0 / (2.0 * np.pi)
TURN_HI = 6.28125
TURN_LO = 2.0 * np.pi - 6.28125
COS = (
    1.0,
    -0.49999988079071045,
    0.041666485369205475,
    -0.0013887786772102118,
    2.476951885910239e-05,
    -2.707541852942086e-07,
    1.7231808202566867e-09,
)

TERM_MAX = 32000.0
TINY = 1e-30


def scaled_cos(angle):
    turns = jnp.round(angle * jnp.float32(TURN))
    rest = (angle - turns * jnp.float32(TURN_HI)) - turns * jnp.float32(TURN_LO)
    square = rest * rest
    value = jnp.float32(COS[-1] * SCALE)
    for c in COS[-2::-1]:
        value = value * square + jnp.float32(c * SCALE)
    return value


def rounded_copies(direction_ref, copies_ref):
    rounded = direction_ref[...].astype(copies_ref.dtype)
    copies_ref[...] = jnp.broadcast_to(rounded[None], copies_ref.shape)


def exchange(blocks, axes):
    return lax.all_to_all(blocks, axes, 0, 0, axis_index_groups=[ORDERS[axes]], tiled=True)


def spread(value, axes):
    n = lax.axis_size(axes)
    copies = jnp.broadcast_to(value[None], (n,) + value.shape)
    return exchange(copies, axes)


def total_of(row, axes):
    return jnp.sum(spread(row, axes), axis=0)


def listed(cols, own):
    cols = jnp.roll(cols, -2, axis=1)
    return jnp.roll(cols, -4 * own, axis=2).reshape(cols.shape[0], -1)


def body(descriptors, freqs, phases, row_weight, resid, coef, direction, ridge, gamma):
    rows_dev, desc = descriptors.shape
    targets = resid.shape[1]
    own = direction.shape[0]
    zl = lax.axis_index("zl")
    swap = [(0, 1), (1, 0)]
    n_plane, n_column = lax.axis_size(PLANE), lax.axis_size(COLUMN)

    def both(mine, peer):
        return jnp.where(zl == 0, jnp.concatenate([mine, peer]), jnp.concatenate([peer, mine]))

    copies = pl.pallas_call(
        rounded_copies,
        out_shape=jax.ShapeDtypeStruct((n_plane, own, targets), jnp.bfloat16),
        cost_estimate=pl.CostEstimate(flops=0, transcendentals=0, bytes_accessed=4 * own * targets + 2 * n_plane * own * targets),
    )(direction)
    copies, descriptors, resid, row_weight, freqs, phases, direction = lax.optimization_barrier(
        (copies, descriptors, resid, row_weight, freqs, phases, direction)
    )
    gathered = exchange(copies, PLANE).reshape(-1, targets)

    rows_x = both(descriptors, lax.ppermute(descriptors, "zl", swap))
    packed = jnp.concatenate([resid, row_weight.reshape(-1, targets)])
    peer = lax.ppermute(packed, "zl", swap)
    rows_resid = both(resid, peer[:rows_dev])
    rows_weight = both(row_weight, peer[rows_dev:].reshape(-1))

    n_x = lax.axis_size("x")
    freq_cols = freqs.reshape(desc, n_x, 2, -1)
    freq_cols = listed(lax.dynamic_index_in_dim(freq_cols, zl, 2, keepdims=False), own)
    phase_cols = lax.dynamic_index_in_dim(phases.reshape(n_x, 2, -1), zl, 1, keepdims=False)
    phase_cols = listed(phase_cols[None], own)[0]
    angle = jnp.dot(rows_x, freq_cols, preferred_element_type=jnp.float32) + phase_cols[None, :]
    feats = scaled_cos(angle).astype(jnp.bfloat16)
    penalty = ridge * jnp.sum(direction * direction, axis=0)
    extra = jnp.broadcast_to(penalty[None, None], (n_column, 8, targets))
    rows_weight = jnp.broadcast_to(rows_weight[:, None], rows_resid.shape)
    resid_size = jnp.sum(jnp.abs(rows_weight * rows_resid), axis=0)
    kind = lax.broadcasted_iota(jnp.int32, (4, targets), 0)
    gathered, feats, rows_resid, rows_weight, extra, resid_size, lower, kind = lax.optimization_barrier(
        (gathered, feats, rows_resid, rows_weight, extra, resid_size, zl == 0, kind)
    )
    partial = jnp.dot(feats, gathered, preferred_element_type=jnp.float32)

    sent = jnp.concatenate([partial.reshape(n_column, -1, targets), extra], axis=1)
    came = jnp.sum(exchange(sent, COLUMN), axis=0)
    share = came.shape[0] - 8
    image = rows_weight * spread(came[:share], COLUMN).reshape(-1, targets)
    local = jnp.where(kind == 0, (jnp.sum(image * image, axis=0) + came[share])[None], resid_size[None])
    local = jnp.where(kind == 2, jnp.sum(jnp.abs(rows_weight * image), axis=0)[None], local)
    seen = spread(local, PLANE)
    alpha = gamma / jnp.sum(seen[:, 0], axis=0)
    bound = jnp.max(seen[:, 1], axis=0) + jnp.abs(alpha) * jnp.max(seen[:, 2], axis=0)
    scale = TERM_MAX / jnp.maximum(SCALE * bound, TINY)
    coef_new = coef + alpha[None, :] * direction
    rows_new = rows_resid - alpha[None, :] * image
    weighted_b = (rows_weight * rows_new).astype(jnp.bfloat16)
    resid_new = jnp.where(lower, rows_new[:rows_dev], rows_new[rows_dev:])
    weighted_b, coef_new = lax.optimization_barrier((weighted_b, coef_new))

    terms = lax.dot_general(
        feats, weighted_b, (((0,), (0,)), ((), ())), preferred_element_type=jnp.float32
    )
    terms = (terms * scale[None, :]).astype(jnp.float16)
    terms = exchange(terms.reshape(n_plane, own, targets), PLANE)
    terms, resid_new = lax.optimization_barrier((terms, resid_new))
    summed = jnp.sum(terms.astype(jnp.float32), axis=0) * (1.0 / scale)[None, :]
    gradient = summed - ridge[None, :] * coef_new
    gamma_new = total_of(total_of(jnp.sum(gradient * gradient, axis=0)[None], COLUMN), PLANE)[0]
    direction_new = gradient + (gamma_new / gamma)[None, :] * direction
    return (coef_new, resid_new, direction_new, gamma_new)


def solution(mesh):
    cut = Mesh(mesh.devices.reshape(SIZES), AXES)
    split = P(FEAT + ROWS, None)
    return jax.shard_map(
        body,
        mesh=cut,
        in_specs=(P(ROWS, None), P(None, FEAT), P(FEAT), P(ROWS), P(ROWS, None), split, split, P(), P()),
        out_specs=(split, P(ROWS, None), split, P()),
        check_vma=False,
    )
```

```python
import jax
import jax.numpy as jnp
import numpy as np
from jax import lax
from jax.experimental import pallas as pl
from jax.sharding import Mesh, PartitionSpec as P

AXES = ("x", "zl", "y", "zh", "core")
SIZES = (4, 2, 8, 4, 2)
ROWS = ("x", "zl", "y")
FEAT = ("zh", "core")
PLANE = ("x", "y")
COLUMN = ("zl", "zh", "core")
LATE_ZL, LATE_ZH = 1, 2

PLANE_ORDER = [((x + 2) % 4) * 8 + (y + 4) % 8 for x in range(4) for y in range(8)]
COLUMN_ORDER = [((i // 8 + LATE_ZL) % 2) * 8 + ((i // 2 + LATE_ZH) % 4) * 2 + i % 2 for i in range(16)]
ORDERS = {PLANE: PLANE_ORDER, COLUMN: COLUMN_ORDER}

SCALE = 2.0**-7
TURN = 1.0 / (2.0 * np.pi)
TURN_HI = 6.28125
TURN_LO = 2.0 * np.pi - 6.28125
COS = (
    1.0,
    -0.49999988079071045,
    0.041666485369205475,
    -0.0013887786772102118,
    2.476951885910239e-05,
    -2.707541852942086e-07,
    1.7231808202566867e-09,
)

TERM_MAX = 32000.0
TINY = 1e-30


def scaled_cos(angle):
    turns = jnp.round(angle * jnp.float32(TURN))
    rest = (angle - turns * jnp.float32(TURN_HI)) - turns * jnp.float32(TURN_LO)
    square = rest * rest
    value = jnp.float32(COS[-1] * SCALE)
    for c in COS[-2::-1]:
        value = value * square + jnp.float32(c * SCALE)
    return value


def first_sends(direction_ref, descriptors_ref, resid_ref, weight_ref, copies_ref, packed_ref):
    rounded = direction_ref[...].astype(copies_ref.dtype)
    copies_ref[...] = jnp.broadcast_to(rounded[None], copies_ref.shape)
    n = resid_ref.shape[0]
    packed_ref[0:n] = descriptors_ref[...].astype(packed_ref.dtype)
    packed_ref[n : 2 * n] = resid_ref[...]
    packed_ref[2 * n :] = weight_ref[...]


def exchange(blocks, axes):
    return lax.all_to_all(blocks, axes, 0, 0, axis_index_groups=[ORDERS[axes]], tiled=True)


def spread(value, axes):
    n = lax.axis_size(axes)
    copies = jnp.broadcast_to(value[None], (n,) + value.shape)
    return exchange(copies, axes)


def total_of(row, axes):
    return jnp.sum(spread(row, axes), axis=0)


def listed(cols, own):
    cols = jnp.roll(cols, -2, axis=1)
    return jnp.roll(cols, -4 * own, axis=2).reshape(cols.shape[0], -1)


def body(descriptors, freqs, phases, row_weight, resid, coef, direction, ridge, gamma):
    rows_dev, desc = descriptors.shape
    targets = resid.shape[1]
    own = direction.shape[0]
    zl = lax.axis_index("zl")
    swap = [(0, 1), (1, 0)]
    n_plane, n_column = lax.axis_size(PLANE), lax.axis_size(COLUMN)

    def both(mine, peer):
        return jnp.where(zl == 0, jnp.concatenate([mine, peer]), jnp.concatenate([peer, mine]))

    weight_rows = row_weight.reshape(-1, targets)
    packed_shape = (2 * rows_dev + weight_rows.shape[0], targets)
    copies, packed = pl.pallas_call(
        first_sends,
        out_shape=(
            jax.ShapeDtypeStruct((n_plane, own, targets), jnp.bfloat16),
            jax.ShapeDtypeStruct(packed_shape, jnp.float32),
        ),
        cost_estimate=pl.CostEstimate(
            flops=0, transcendentals=0, bytes_accessed=2 * n_plane * own * targets + 8 * packed_shape[0] * targets
        ),
    )(direction, descriptors, resid, weight_rows)
    copies, packed, descriptors, resid, row_weight, freqs, phases, direction = lax.optimization_barrier(
        (copies, packed, descriptors, resid, row_weight, freqs, phases, direction)
    )
    gathered = exchange(copies, PLANE).reshape(-1, targets)

    peer = lax.ppermute(packed, "zl", swap)
    rows_x = both(descriptors, peer[:rows_dev].astype(jnp.bfloat16))
    rows_resid = both(resid, peer[rows_dev : 2 * rows_dev])
    rows_weight = both(row_weight, peer[2 * rows_dev :].reshape(-1))

    n_x = lax.axis_size("x")
    freq_cols = freqs.reshape(desc, n_x, 2, -1)
    freq_cols = listed(lax.dynamic_index_in_dim(freq_cols, zl, 2, keepdims=False), own)
    phase_cols = lax.dynamic_index_in_dim(phases.reshape(n_x, 2, -1), zl, 1, keepdims=False)
    phase_cols = listed(phase_cols[None], own)[0]
    angle = jnp.dot(rows_x, freq_cols, preferred_element_type=jnp.float32) + phase_cols[None, :]
    feats = scaled_cos(angle).astype(jnp.bfloat16)
    penalty = ridge * jnp.sum(direction * direction, axis=0)
    extra = jnp.broadcast_to(penalty[None, None], (n_column, 8, targets))
    rows_weight = jnp.broadcast_to(rows_weight[:, None], rows_resid.shape)
    resid_size = jnp.sum(jnp.abs(rows_weight * rows_resid), axis=0)
    kind = lax.broadcasted_iota(jnp.int32, (4, targets), 0)
    gathered, feats, rows_resid, rows_weight, extra, resid_size, lower, kind = lax.optimization_barrier(
        (gathered, feats, rows_resid, rows_weight, extra, resid_size, zl == 0, kind)
    )
    partial = jnp.dot(feats, gathered, preferred_element_type=jnp.float32)

    sent = jnp.concatenate([partial.reshape(n_column, -1, targets), extra], axis=1)
    came = jnp.sum(exchange(sent, COLUMN), axis=0)
    share = came.shape[0] - 8
    image = rows_weight * spread(came[:share], COLUMN).reshape(-1, targets)
    local = jnp.where(kind == 0, (jnp.sum(image * image, axis=0) + came[share])[None], resid_size[None])
    local = jnp.where(kind == 2, jnp.sum(jnp.abs(rows_weight * image), axis=0)[None], local)
    seen = spread(local, PLANE)
    alpha = gamma / jnp.sum(seen[:, 0], axis=0)
    bound = jnp.max(seen[:, 1], axis=0) + jnp.abs(alpha) * jnp.max(seen[:, 2], axis=0)
    scale = TERM_MAX / jnp.maximum(SCALE * bound, TINY)
    coef_new = coef + alpha[None, :] * direction
    rows_new = rows_resid - alpha[None, :] * image
    weighted_b = (rows_weight * rows_new).astype(jnp.bfloat16)
    resid_new = jnp.where(lower, rows_new[:rows_dev], rows_new[rows_dev:])
    weighted_b, coef_new = lax.optimization_barrier((weighted_b, coef_new))

    terms = lax.dot_general(
        feats, weighted_b, (((0,), (0,)), ((), ())), preferred_element_type=jnp.float32
    )
    terms = (terms * scale[None, :]).astype(jnp.float16)
    terms = exchange(terms.reshape(n_plane, own, targets), PLANE)
    terms, resid_new = lax.optimization_barrier((terms, resid_new))
    summed = jnp.sum(terms.astype(jnp.float32), axis=0) * (1.0 / scale)[None, :]
    gradient = summed - ridge[None, :] * coef_new
    gamma_new = total_of(total_of(jnp.sum(gradient * gradient, axis=0)[None], COLUMN), PLANE)[0]
    direction_new = gradient + (gamma_new / gamma)[None, :] * direction
    return (coef_new, resid_new, direction_new, gamma_new)


def solution(mesh):
    cut = Mesh(mesh.devices.reshape(SIZES), AXES)
    split = P(FEAT + ROWS, None)
    return jax.shard_map(
        body,
        mesh=cut,
        in_specs=(P(ROWS, None), P(None, FEAT), P(FEAT), P(ROWS), P(ROWS, None), split, split, P(), P()),
        out_specs=(split, P(ROWS, None), split, P()),
        check_vma=False,
    )
```

```python
import jax
import jax.numpy as jnp
import numpy as np
from jax import lax
from jax.experimental import pallas as pl
from jax.sharding import Mesh, PartitionSpec as P

AXES = ("x", "zl", "y", "zh", "core")
SIZES = (4, 2, 8, 4, 2)
ROWS = ("x", "zl", "y")
FEAT = ("zh", "core")
PLANE = ("x", "y")
COLUMN = ("zl", "zh", "core")
LATE_ZL, LATE_ZH = 1, 2

PLANE_ORDER = [((x + 2) % 4) * 8 + (y + 4) % 8 for x in range(4) for y in range(8)]
COLUMN_ORDER = [((i // 8 + LATE_ZL) % 2) * 8 + ((i // 2 + LATE_ZH) % 4) * 2 + i % 2 for i in range(16)]
ORDERS = {PLANE: PLANE_ORDER, COLUMN: COLUMN_ORDER}

SCALE = 2.0**-7
TURN = 1.0 / (2.0 * np.pi)
TURN_HI = 6.28125
TURN_LO = 2.0 * np.pi - 6.28125
COS = (
    1.0,
    -0.49999988079071045,
    0.041666485369205475,
    -0.0013887786772102118,
    2.476951885910239e-05,
    -2.707541852942086e-07,
    1.7231808202566867e-09,
)

TERM_MAX = 32000.0
TINY = 1e-30


def scaled_cos(angle):
    turns = jnp.round(angle * jnp.float32(TURN))
    rest = (angle - turns * jnp.float32(TURN_HI)) - turns * jnp.float32(TURN_LO)
    square = rest * rest
    value = jnp.float32(COS[-1] * SCALE)
    for c in COS[-2::-1]:
        value = value * square + jnp.float32(c * SCALE)
    return value


def rounded_copies(direction_ref, copies_ref):
    rounded = direction_ref[...].astype(copies_ref.dtype)
    copies_ref[...] = jnp.broadcast_to(rounded[None], copies_ref.shape)


def exchange(blocks, axes):
    return lax.all_to_all(blocks, axes, 0, 0, axis_index_groups=[ORDERS[axes]], tiled=True)


def spread(value, axes):
    n = lax.axis_size(axes)
    copies = jnp.broadcast_to(value[None], (n,) + value.shape)
    return exchange(copies, axes)


def total_of(row, axes):
    return jnp.sum(spread(row, axes), axis=0)


def listed(cols, own):
    cols = jnp.roll(cols, -2, axis=1)
    return jnp.roll(cols, -4 * own, axis=2).reshape(cols.shape[0], -1)


def body(descriptors, freqs, phases, row_weight, resid, coef, direction, ridge, gamma):
    rows_dev, desc = descriptors.shape
    targets = resid.shape[1]
    own = direction.shape[0]
    zl = lax.axis_index("zl")
    swap = [(0, 1), (1, 0)]
    n_plane, n_column = lax.axis_size(PLANE), lax.axis_size(COLUMN)

    def both(mine, peer):
        return jnp.where(zl == 0, jnp.concatenate([mine, peer]), jnp.concatenate([peer, mine]))

    copies = pl.pallas_call(
        rounded_copies,
        out_shape=jax.ShapeDtypeStruct((n_plane, own, targets), jnp.bfloat16),
        cost_estimate=pl.CostEstimate(flops=0, transcendentals=0, bytes_accessed=4 * own * targets + 2 * n_plane * own * targets),
    )(direction)
    copies, descriptors, resid, row_weight, freqs, phases, direction = lax.optimization_barrier(
        (copies, descriptors, resid, row_weight, freqs, phases, direction)
    )
    gathered = exchange(copies, PLANE).reshape(-1, targets)

    rows_x = both(descriptors, lax.ppermute(descriptors, "zl", swap))
    packed = jnp.concatenate([resid, row_weight.reshape(-1, targets)])
    peer = lax.ppermute(packed, "zl", swap)
    own_resid, peer_resid = resid, peer[:rows_dev]
    rows_weight = both(row_weight, peer[rows_dev:].reshape(-1))

    n_x = lax.axis_size("x")
    freq_cols = freqs.reshape(desc, n_x, 2, -1)
    freq_cols = listed(lax.dynamic_index_in_dim(freq_cols, zl, 2, keepdims=False), own)
    phase_cols = lax.dynamic_index_in_dim(phases.reshape(n_x, 2, -1), zl, 1, keepdims=False)
    phase_cols = listed(phase_cols[None], own)[0]
    angle = jnp.dot(rows_x, freq_cols, preferred_element_type=jnp.float32) + phase_cols[None, :]
    feats = scaled_cos(angle).astype(jnp.bfloat16)
    penalty = ridge * jnp.sum(direction * direction, axis=0)
    extra = jnp.broadcast_to(penalty[None, None], (n_column, 8, targets))
    rows_weight = jnp.broadcast_to(rows_weight[:, None], (2 * rows_dev, targets))
    resid_size = jnp.sum(jnp.abs(rows_weight * both(own_resid, peer_resid)), axis=0)
    kind = lax.broadcasted_iota(jnp.int32, (4, targets), 0)
    gathered, feats, own_resid, peer_resid, rows_weight, extra, resid_size, lower, kind = lax.optimization_barrier(
        (gathered, feats, own_resid, peer_resid, rows_weight, extra, resid_size, zl == 0, kind)
    )
    partial = jnp.dot(feats, gathered, preferred_element_type=jnp.float32)

    sent = jnp.concatenate([partial.reshape(n_column, -1, targets), extra], axis=1)
    came = jnp.sum(exchange(sent, COLUMN), axis=0)
    share = came.shape[0] - 8
    image = rows_weight * spread(came[:share], COLUMN).reshape(-1, targets)
    local = jnp.where(kind == 0, (jnp.sum(image * image, axis=0) + came[share])[None], resid_size[None])
    local = jnp.where(kind == 2, jnp.sum(jnp.abs(rows_weight * image), axis=0)[None], local)
    seen = spread(local, PLANE)
    alpha = gamma / jnp.sum(seen[:, 0], axis=0)
    bound = jnp.max(seen[:, 1], axis=0) + jnp.abs(alpha) * jnp.max(seen[:, 2], axis=0)
    scale = TERM_MAX / jnp.maximum(SCALE * bound, TINY)
    coef_new = coef + alpha[None, :] * direction
    own_image = jnp.where(lower, image[:rows_dev], image[rows_dev:])
    peer_image = jnp.where(lower, image[rows_dev:], image[:rows_dev])
    resid_new = lax.optimization_barrier(own_resid - alpha[None, :] * own_image)
    peer_new = peer_resid - alpha[None, :] * peer_image
    rows_new = jnp.where(lower, jnp.concatenate([resid_new, peer_new]), jnp.concatenate([peer_new, resid_new]))
    weighted_b = (rows_weight * rows_new).astype(jnp.bfloat16)
    weighted_b, coef_new, resid_new = lax.optimization_barrier((weighted_b, coef_new, resid_new))

    terms = lax.dot_general(
        feats, weighted_b, (((0,), (0,)), ((), ())), preferred_element_type=jnp.float32
    )
    terms = (terms * scale[None, :]).astype(jnp.float16)
    terms = exchange(terms.reshape(n_plane, own, targets), PLANE)
    summed = jnp.sum(terms.astype(jnp.float32), axis=0) * (1.0 / scale)[None, :]
    gradient = summed - ridge[None, :] * coef_new
    gamma_new = total_of(total_of(jnp.sum(gradient * gradient, axis=0)[None], COLUMN), PLANE)[0]
    direction_new = gradient + (gamma_new / gamma)[None, :] * direction
    return (coef_new, resid_new, direction_new, gamma_new)


def solution(mesh):
    cut = Mesh(mesh.devices.reshape(SIZES), AXES)
    split = P(FEAT + ROWS, None)
    return jax.shard_map(
        body,
        mesh=cut,
        in_specs=(P(ROWS, None), P(None, FEAT), P(FEAT), P(ROWS), P(ROWS, None), split, split, P(), P()),
        out_specs=(split, P(ROWS, None), split, P()),
        check_vma=False,
    )
```

```python
import jax
import jax.numpy as jnp
import numpy as np
from jax import lax
from jax.experimental import pallas as pl
from jax.sharding import Mesh, PartitionSpec as P

AXES = ("x", "zl", "y", "zh", "core")
SIZES = (4, 2, 8, 4, 2)
ROWS = ("x", "zl", "y")
FEAT = ("zh", "core")
PLANE = ("x", "y")
COLUMN = ("zl", "zh", "core")
LATE_ZL, LATE_ZH = 1, 2

PLANE_ORDER = [((x + 2) % 4) * 8 + (y + 4) % 8 for x in range(4) for y in range(8)]
COLUMN_ORDER = [((i // 8 + LATE_ZL) % 2) * 8 + ((i // 2 + LATE_ZH) % 4) * 2 + i % 2 for i in range(16)]
ORDERS = {PLANE: PLANE_ORDER, COLUMN: COLUMN_ORDER}

SCALE = 2.0**-7
TURN = 1.0 / (2.0 * np.pi)
TURN_HI = 6.28125
TURN_LO = 2.0 * np.pi - 6.28125
COS = (
    1.0,
    -0.49999988079071045,
    0.041666485369205475,
    -0.0013887786772102118,
    2.476951885910239e-05,
    -2.707541852942086e-07,
    1.7231808202566867e-09,
)

TERM_MAX = 32000.0
TINY = 1e-30


def scaled_cos(angle):
    turns = jnp.round(angle * jnp.float32(TURN))
    rest = (angle - turns * jnp.float32(TURN_HI)) - turns * jnp.float32(TURN_LO)
    square = rest * rest
    value = jnp.float32(COS[-1] * SCALE)
    for c in COS[-2::-1]:
        value = value * square + jnp.float32(c * SCALE)
    return value


def first_sends(direction_ref, descriptors_ref, resid_ref, weight_ref, copies_ref, packed_ref):
    rounded = direction_ref[...].astype(copies_ref.dtype)
    copies_ref[...] = jnp.broadcast_to(rounded[None], copies_ref.shape)
    n = resid_ref.shape[0]
    packed_ref[0:n] = descriptors_ref[...].astype(packed_ref.dtype)
    packed_ref[n : 2 * n] = resid_ref[...]
    packed_ref[2 * n :] = weight_ref[...]


def exchange(blocks, axes):
    return lax.all_to_all(blocks, axes, 0, 0, axis_index_groups=[ORDERS[axes]], tiled=True)


def spread(value, axes):
    n = lax.axis_size(axes)
    copies = jnp.broadcast_to(value[None], (n,) + value.shape)
    return exchange(copies, axes)


def total_of(row, axes):
    return jnp.sum(spread(row, axes), axis=0)


def listed(cols, own):
    cols = jnp.roll(cols, -2, axis=1)
    return jnp.roll(cols, -4 * own, axis=2).reshape(cols.shape[0], -1)


def body(descriptors, freqs, phases, row_weight, resid, coef, direction, ridge, gamma):
    rows_dev, desc = descriptors.shape
    targets = resid.shape[1]
    own = direction.shape[0]
    zl = lax.axis_index("zl")
    lower = zl == 0
    swap = [(0, 1), (1, 0)]
    n_plane, n_column = lax.axis_size(PLANE), lax.axis_size(COLUMN)

    def halves(first, second):
        return jnp.where(lower, first, second), jnp.where(lower, second, first)

    weight_rows = row_weight.reshape(-1, targets)
    packed_shape = (2 * rows_dev + weight_rows.shape[0], targets)
    copies, packed = pl.pallas_call(
        first_sends,
        out_shape=(
            jax.ShapeDtypeStruct((n_plane, own, targets), jnp.bfloat16),
            jax.ShapeDtypeStruct(packed_shape, jnp.float32),
        ),
        cost_estimate=pl.CostEstimate(
            flops=0, transcendentals=0, bytes_accessed=2 * n_plane * own * targets + 8 * packed_shape[0] * targets
        ),
    )(direction, descriptors, resid, weight_rows)
    copies, packed, descriptors, resid, row_weight, freqs, phases, direction = lax.optimization_barrier(
        (copies, packed, descriptors, resid, row_weight, freqs, phases, direction)
    )
    gathered = exchange(copies, PLANE).reshape(-1, targets)

    peer = lax.ppermute(packed, "zl", swap)
    peer_x = peer[:rows_dev].astype(jnp.bfloat16)
    peer_resid = peer[rows_dev : 2 * rows_dev]

    n_x = lax.axis_size("x")
    freq_cols = freqs.reshape(desc, n_x, 2, -1)
    freq_cols = listed(lax.dynamic_index_in_dim(freq_cols, zl, 2, keepdims=False), own)
    phase_cols = lax.dynamic_index_in_dim(phases.reshape(n_x, 2, -1), zl, 1, keepdims=False)
    phase_cols = listed(phase_cols[None], own)[0]

    def features(block_x):
        angle = jnp.dot(block_x, freq_cols, preferred_element_type=jnp.float32) + phase_cols[None, :]
        return scaled_cos(angle).astype(jnp.bfloat16)

    own_feats = features(descriptors)
    peer_feats = features(peer_x)
    penalty = ridge * jnp.sum(direction * direction, axis=0)
    extra = jnp.broadcast_to(penalty[None, None], (n_column, 8, targets))
    own_weight = jnp.broadcast_to(row_weight[:, None], resid.shape)
    peer_weight = jnp.broadcast_to(peer[2 * rows_dev :].reshape(-1)[:, None], resid.shape)
    resid_size = jnp.sum(jnp.abs(own_weight * resid), axis=0) + jnp.sum(jnp.abs(peer_weight * peer_resid), axis=0)
    kind = lax.broadcasted_iota(jnp.int32, (4, targets), 0)
    (gathered, own_feats, peer_feats, own_resid, peer_resid, own_weight, peer_weight, extra, resid_size, lower, kind) = (
        lax.optimization_barrier(
            (gathered, own_feats, peer_feats, resid, peer_resid, own_weight, peer_weight, extra, resid_size, lower, kind)
        )
    )
    partial = halves(
        jnp.dot(own_feats, gathered, preferred_element_type=jnp.float32),
        jnp.dot(peer_feats, gathered, preferred_element_type=jnp.float32),
    )
    partial = jnp.concatenate(partial)

    sent = jnp.concatenate([partial.reshape(n_column, -1, targets), extra], axis=1)
    came = jnp.sum(exchange(sent, COLUMN), axis=0)
    share = came.shape[0] - 8
    rows = spread(came[:share], COLUMN).reshape(-1, targets)
    own_image, peer_image = halves(rows[:rows_dev], rows[rows_dev:])
    own_image, peer_image = own_weight * own_image, peer_weight * peer_image
    squares = jnp.sum(own_image * own_image + peer_image * peer_image, axis=0)
    image_size = jnp.sum(jnp.abs(own_weight * own_image) + jnp.abs(peer_weight * peer_image), axis=0)
    local = jnp.where(kind == 0, (squares + came[share])[None], resid_size[None])
    local = jnp.where(kind == 2, image_size[None], local)
    seen = spread(local, PLANE)
    alpha = gamma / jnp.sum(seen[:, 0], axis=0)
    bound = jnp.max(seen[:, 1], axis=0) + jnp.abs(alpha) * jnp.max(seen[:, 2], axis=0)
    scale = TERM_MAX / jnp.maximum(SCALE * bound, TINY)
    coef_new = coef + alpha[None, :] * direction
    resid_new = lax.optimization_barrier(own_resid - alpha[None, :] * own_image)
    own_b = (own_weight * resid_new).astype(jnp.bfloat16)
    peer_b = (peer_weight * (peer_resid - alpha[None, :] * peer_image)).astype(jnp.bfloat16)
    own_b, peer_b, coef_new, resid_new = lax.optimization_barrier((own_b, peer_b, coef_new, resid_new))

    def down(feats, weighted_b):
        return lax.dot_general(feats, weighted_b, (((0,), (0,)), ((), ())), preferred_element_type=jnp.float32)

    terms = down(own_feats, own_b) + down(peer_feats, peer_b)
    terms = (terms * scale[None, :]).astype(jnp.float16)
    terms = exchange(terms.reshape(n_plane, own, targets), PLANE)
    summed = jnp.sum(terms.astype(jnp.float32), axis=0) * (1.0 / scale)[None, :]
    gradient = summed - ridge[None, :] * coef_new
    gamma_new = total_of(total_of(jnp.sum(gradient * gradient, axis=0)[None], COLUMN), PLANE)[0]
    direction_new = gradient + (gamma_new / gamma)[None, :] * direction
    return (coef_new, resid_new, direction_new, gamma_new)


def solution(mesh):
    cut = Mesh(mesh.devices.reshape(SIZES), AXES)
    split = P(FEAT + ROWS, None)
    return jax.shard_map(
        body,
        mesh=cut,
        in_specs=(P(ROWS, None), P(None, FEAT), P(FEAT), P(ROWS), P(ROWS, None), split, split, P(), P()),
        out_specs=(split, P(ROWS, None), split, P()),
        check_vma=False,
    )
```

```python
import jax
import jax.numpy as jnp
import numpy as np
from jax import lax
from jax.experimental import pallas as pl
from jax.sharding import Mesh, PartitionSpec as P

AXES = ("x", "zl", "y", "zh", "core")
SIZES = (4, 2, 8, 4, 2)
ROWS = ("x", "zl", "y")
FEAT = ("zh", "core")
PLANE = ("x", "y")
COLUMN = ("zl", "zh", "core")
LATE_ZL, LATE_ZH = 1, 2

PLANE_ORDER = [((x + 2) % 4) * 8 + (y + 4) % 8 for x in range(4) for y in range(8)]
COLUMN_ORDER = [((i // 8 + LATE_ZL) % 2) * 8 + ((i // 2 + LATE_ZH) % 4) * 2 + i % 2 for i in range(16)]
ORDERS = {PLANE: PLANE_ORDER, COLUMN: COLUMN_ORDER}

SCALE = 2.0**-7
TURN = 1.0 / (2.0 * np.pi)
TURN_HI = 6.28125
TURN_LO = 2.0 * np.pi - 6.28125
COS = (
    1.0,
    -0.49999988079071045,
    0.041666485369205475,
    -0.0013887786772102118,
    2.476951885910239e-05,
    -2.707541852942086e-07,
    1.7231808202566867e-09,
)

TERM_MAX = 32000.0
TINY = 1e-30


def scaled_cos(angle):
    turns = jnp.round(angle * jnp.float32(TURN))
    rest = (angle - turns * jnp.float32(TURN_HI)) - turns * jnp.float32(TURN_LO)
    square = rest * rest
    value = jnp.float32(COS[-1] * SCALE)
    for c in COS[-2::-1]:
        value = value * square + jnp.float32(c * SCALE)
    return value


def rounded_copies(direction_ref, copies_ref):
    rounded = direction_ref[...].astype(copies_ref.dtype)
    copies_ref[...] = jnp.broadcast_to(rounded[None], copies_ref.shape)


def exchange(blocks, axes):
    return lax.all_to_all(blocks, axes, 0, 0, axis_index_groups=[ORDERS[axes]], tiled=True)


def spread(value, axes):
    n = lax.axis_size(axes)
    copies = jnp.broadcast_to(value[None], (n,) + value.shape)
    return exchange(copies, axes)


def total_of(row, axes):
    return jnp.sum(spread(row, axes), axis=0)


def listed(cols, own):
    cols = jnp.roll(cols, -2, axis=1)
    return jnp.roll(cols, -4 * own, axis=2).reshape(cols.shape[0], -1)


def body(descriptors, freqs, phases, row_weight, resid, coef, direction, ridge, gamma):
    rows_dev, desc = descriptors.shape
    targets = resid.shape[1]
    own = direction.shape[0]
    zl = lax.axis_index("zl")
    swap = [(0, 1), (1, 0)]
    n_plane, n_column = lax.axis_size(PLANE), lax.axis_size(COLUMN)

    def both(mine, peer):
        return jnp.where(zl == 0, jnp.concatenate([mine, peer]), jnp.concatenate([peer, mine]))

    copies = pl.pallas_call(
        rounded_copies,
        out_shape=jax.ShapeDtypeStruct((n_plane, own, targets), jnp.bfloat16),
        cost_estimate=pl.CostEstimate(flops=0, transcendentals=0, bytes_accessed=4 * own * targets + 2 * n_plane * own * targets),
    )(direction)
    copies, descriptors, resid, row_weight, freqs, phases, direction = lax.optimization_barrier(
        (copies, descriptors, resid, row_weight, freqs, phases, direction)
    )
    gathered = exchange(copies, PLANE).reshape(-1, targets)

    rows_x = both(descriptors, lax.ppermute(descriptors, "zl", swap))
    packed = jnp.concatenate([resid, row_weight.reshape(-1, targets)])
    peer = lax.ppermute(packed, "zl", swap)
    rows_resid = both(resid, peer[:rows_dev])
    rows_weight = both(row_weight, peer[rows_dev:].reshape(-1))

    n_x = lax.axis_size("x")
    freq_cols = freqs.reshape(desc, n_x, 2, -1)
    freq_cols = listed(lax.dynamic_index_in_dim(freq_cols, zl, 2, keepdims=False), own)
    phase_cols = lax.dynamic_index_in_dim(phases.reshape(n_x, 2, -1), zl, 1, keepdims=False)
    phase_cols = listed(phase_cols[None], own)[0]
    angle = jnp.dot(rows_x, freq_cols, preferred_element_type=jnp.float32) + phase_cols[None, :]
    feats = scaled_cos(angle).astype(jnp.bfloat16)
    penalty = ridge * jnp.sum(direction * direction, axis=0)
    extra = jnp.broadcast_to(penalty[None, None], (n_column, 8, targets))
    rows_weight = jnp.broadcast_to(rows_weight[:, None], (2 * rows_dev, targets))
    resid_size = jnp.sum(jnp.abs(rows_weight * rows_resid), axis=0)
    kind = lax.broadcasted_iota(jnp.int32, (4, targets), 0)
    gathered, feats, rows_resid, rows_weight, extra, resid_size, lower, kind = lax.optimization_barrier(
        (gathered, feats, rows_resid, rows_weight, extra, resid_size, zl == 0, kind)
    )
    partial = jnp.dot(feats, gathered, preferred_element_type=jnp.float32)

    sent = jnp.concatenate([partial.reshape(n_column, -1, targets), extra], axis=1)
    came = jnp.sum(exchange(sent, COLUMN), axis=0)
    share = came.shape[0] - 8
    image = rows_weight * spread(came[:share], COLUMN).reshape(-1, targets)
    local = jnp.where(kind == 0, (jnp.sum(image * image, axis=0) + came[share])[None], resid_size[None])
    local = jnp.where(kind == 2, jnp.sum(jnp.abs(rows_weight * image), axis=0)[None], local)
    seen = spread(local, PLANE)
    alpha = gamma / jnp.sum(seen[:, 0], axis=0)
    bound = jnp.max(seen[:, 1], axis=0) + jnp.abs(alpha) * jnp.max(seen[:, 2], axis=0)
    scale = TERM_MAX / jnp.maximum(SCALE * bound, TINY)
    coef_new = coef + alpha[None, :] * direction
    rows_new = rows_resid - alpha[None, :] * image
    resid_new = lax.optimization_barrier(jnp.where(lower, rows_new[:rows_dev], rows_new[rows_dev:]))
    peer_new = jnp.where(lower, rows_new[rows_dev:], rows_new[:rows_dev])
    rows_new = jnp.where(lower, jnp.concatenate([resid_new, peer_new]), jnp.concatenate([peer_new, resid_new]))
    weighted_b = (rows_weight * rows_new).astype(jnp.bfloat16)
    weighted_b, coef_new, resid_new = lax.optimization_barrier((weighted_b, coef_new, resid_new))

    terms = lax.dot_general(
        feats, weighted_b, (((0,), (0,)), ((), ())), preferred_element_type=jnp.float32
    )
    terms = (terms * scale[None, :]).astype(jnp.float16)
    terms = exchange(terms.reshape(n_plane, own, targets), PLANE)
    summed = jnp.sum(terms.astype(jnp.float32), axis=0) * (1.0 / scale)[None, :]
    gradient = summed - ridge[None, :] * coef_new
    gamma_new = total_of(total_of(jnp.sum(gradient * gradient, axis=0)[None], COLUMN), PLANE)[0]
    direction_new = gradient + (gamma_new / gamma)[None, :] * direction
    return (coef_new, resid_new, direction_new, gamma_new)


def solution(mesh):
    cut = Mesh(mesh.devices.reshape(SIZES), AXES)
    split = P(FEAT + ROWS, None)
    return jax.shard_map(
        body,
        mesh=cut,
        in_specs=(P(ROWS, None), P(None, FEAT), P(FEAT), P(ROWS), P(ROWS, None), split, split, P(), P()),
        out_specs=(split, P(ROWS, None), split, P()),
        check_vma=False,
    )
```

```python
import jax
import jax.numpy as jnp
import numpy as np
from jax import lax
from jax.sharding import Mesh, PartitionSpec as P

AXES = ("x", "zl", "y", "zh", "core")
SIZES = (4, 2, 8, 4, 2)
ROWS = ("x", "zl", "y")
FEAT = ("zh", "core")
PLANE = ("x", "y")
COLUMN = ("zl", "zh", "core")
LATE_ZL, LATE_ZH = 1, 2

PLANE_ORDER = [((x + 2) % 4) * 8 + (y + 4) % 8 for x in range(4) for y in range(8)]
COLUMN_ORDER = [((i // 8 + LATE_ZL) % 2) * 8 + ((i // 2 + LATE_ZH) % 4) * 2 + i % 2 for i in range(16)]
ORDERS = {PLANE: PLANE_ORDER, COLUMN: COLUMN_ORDER}

SCALE = 2.0**-7
TURN = 1.0 / (2.0 * np.pi)
TURN_HI = 6.28125
TURN_LO = 2.0 * np.pi - 6.28125
COS = (
    1.0,
    -0.49999988079071045,
    0.041666485369205475,
    -0.0013887786772102118,
    2.476951885910239e-05,
    -2.707541852942086e-07,
    1.7231808202566867e-09,
)

TERM_MAX = 32000.0
TINY = 1e-30


def scaled_cos(angle):
    turns = jnp.round(angle * jnp.float32(TURN))
    rest = (angle - turns * jnp.float32(TURN_HI)) - turns * jnp.float32(TURN_LO)
    square = rest * rest
    value = jnp.float32(COS[-1] * SCALE)
    for c in COS[-2::-1]:
        value = value * square + jnp.float32(c * SCALE)
    return value


def exchange(blocks, axes):
    return lax.all_to_all(blocks, axes, 0, 0, axis_index_groups=[ORDERS[axes]], tiled=True)


def spread(value, axes):
    n = lax.axis_size(axes)
    copies = jnp.broadcast_to(value[None], (n,) + value.shape)
    return exchange(copies, axes)


def total_of(row, axes):
    return jnp.sum(spread(row, axes), axis=0)


def listed(cols, own):
    cols = jnp.roll(cols, -2, axis=1)
    return jnp.roll(cols, -4 * own, axis=2).reshape(cols.shape[0], -1)


def body(descriptors, freqs, phases, row_weight, resid, coef, direction, ridge, gamma):
    rows_dev, desc = descriptors.shape
    targets = resid.shape[1]
    own = direction.shape[0]
    zl = lax.axis_index("zl")
    swap = [(0, 1), (1, 0)]
    n_plane, n_column = lax.axis_size(PLANE), lax.axis_size(COLUMN)

    def both(mine, peer):
        return jnp.where(zl == 0, jnp.concatenate([mine, peer]), jnp.concatenate([peer, mine]))

    every = lax.broadcasted_iota(jnp.int32, (n_plane, own, targets), 0) >= -zl
    copies = jnp.where(every, direction[None], 0.0).astype(jnp.bfloat16)
    copies, descriptors, resid, row_weight, freqs, phases, direction = lax.optimization_barrier(
        (copies, descriptors, resid, row_weight, freqs, phases, direction)
    )
    gathered = exchange(copies, PLANE).reshape(-1, targets)

    rows_x = both(descriptors, lax.ppermute(descriptors, "zl", swap))
    packed = jnp.concatenate([resid, row_weight.reshape(-1, targets)])
    peer = lax.ppermute(packed, "zl", swap)
    rows_resid = both(resid, peer[:rows_dev])
    rows_weight = both(row_weight, peer[rows_dev:].reshape(-1))

    n_x = lax.axis_size("x")
    freq_cols = freqs.reshape(desc, n_x, 2, -1)
    freq_cols = listed(lax.dynamic_index_in_dim(freq_cols, zl, 2, keepdims=False), own)
    phase_cols = lax.dynamic_index_in_dim(phases.reshape(n_x, 2, -1), zl, 1, keepdims=False)
    phase_cols = listed(phase_cols[None], own)[0]
    angle = jnp.dot(rows_x, freq_cols, preferred_element_type=jnp.float32) + phase_cols[None, :]
    feats = scaled_cos(angle).astype(jnp.bfloat16)
    penalty = ridge * jnp.sum(direction * direction, axis=0)
    extra = jnp.broadcast_to(penalty[None, None], (n_column, 8, targets))
    rows_weight = jnp.broadcast_to(rows_weight[:, None], (2 * rows_dev, targets))
    resid_size = jnp.sum(jnp.abs(rows_weight * rows_resid), axis=0)
    kind = lax.broadcasted_iota(jnp.int32, (4, targets), 0)
    gathered, feats, rows_resid, rows_weight, extra, resid_size, lower, kind = lax.optimization_barrier(
        (gathered, feats, rows_resid, rows_weight, extra, resid_size, zl == 0, kind)
    )
    partial = jnp.dot(feats, gathered, preferred_element_type=jnp.float32)

    sent = jnp.concatenate([partial.reshape(n_column, -1, targets), extra], axis=1)
    came = jnp.sum(exchange(sent, COLUMN), axis=0)
    share = came.shape[0] - 8
    image = rows_weight * spread(came[:share], COLUMN).reshape(-1, targets)
    local = jnp.where(kind == 0, (jnp.sum(image * image, axis=0) + came[share])[None], resid_size[None])
    local = jnp.where(kind == 2, jnp.sum(jnp.abs(rows_weight * image), axis=0)[None], local)
    seen = spread(local, PLANE)
    alpha = gamma / jnp.sum(seen[:, 0], axis=0)
    bound = jnp.max(seen[:, 1], axis=0) + jnp.abs(alpha) * jnp.max(seen[:, 2], axis=0)
    scale = TERM_MAX / jnp.maximum(SCALE * bound, TINY)
    coef_new = coef + alpha[None, :] * direction
    rows_new = rows_resid - alpha[None, :] * image
    resid_new = lax.optimization_barrier(jnp.where(lower, rows_new[:rows_dev], rows_new[rows_dev:]))
    peer_new = jnp.where(lower, rows_new[rows_dev:], rows_new[:rows_dev])
    rows_new = jnp.where(lower, jnp.concatenate([resid_new, peer_new]), jnp.concatenate([peer_new, resid_new]))
    weighted_b = (rows_weight * rows_new).astype(jnp.bfloat16)
    weighted_b, coef_new, resid_new = lax.optimization_barrier((weighted_b, coef_new, resid_new))

    terms = lax.dot_general(
        feats, weighted_b, (((0,), (0,)), ((), ())), preferred_element_type=jnp.float32
    )
    terms = (terms * scale[None, :]).astype(jnp.float16)
    terms = exchange(terms.reshape(n_plane, own, targets), PLANE)
    summed = jnp.sum(terms.astype(jnp.float32), axis=0) * (1.0 / scale)[None, :]
    gradient = summed - ridge[None, :] * coef_new
    gamma_new = total_of(total_of(jnp.sum(gradient * gradient, axis=0)[None], COLUMN), PLANE)[0]
    direction_new = gradient + (gamma_new / gamma)[None, :] * direction
    return (coef_new, resid_new, direction_new, gamma_new)


def solution(mesh):
    cut = Mesh(mesh.devices.reshape(SIZES), AXES)
    split = P(FEAT + ROWS, None)
    return jax.shard_map(
        body,
        mesh=cut,
        in_specs=(P(ROWS, None), P(None, FEAT), P(FEAT), P(ROWS), P(ROWS, None), split, split, P(), P()),
        out_specs=(split, P(ROWS, None), split, P()),
        check_vma=False,
    )
```

```python
import jax
import jax.numpy as jnp
import numpy as np
from jax import lax
from jax.experimental import pallas as pl
from jax.sharding import Mesh, PartitionSpec as P

AXES = ("x", "zl", "y", "zh", "core")
SIZES = (4, 2, 8, 4, 2)
ROWS = ("x", "zl", "y")
FEAT = ("zh", "core")
PLANE = ("x", "y")
COLUMN = ("zl", "zh", "core")
LATE_ZL, LATE_ZH = 1, 2

PLANE_ORDER = [((x + 2) % 4) * 8 + (y + 4) % 8 for x in range(4) for y in range(8)]
COLUMN_ORDER = [((i // 8 + LATE_ZL) % 2) * 8 + ((i // 2 + LATE_ZH) % 4) * 2 + i % 2 for i in range(16)]
ORDERS = {PLANE: PLANE_ORDER, COLUMN: COLUMN_ORDER}

SCALE = 2.0**-7
TURN = 1.0 / (2.0 * np.pi)
TURN_HI = 6.28125
TURN_LO = 2.0 * np.pi - 6.28125
COS = (
    1.0,
    -0.49999988079071045,
    0.041666485369205475,
    -0.0013887786772102118,
    2.476951885910239e-05,
    -2.707541852942086e-07,
    1.7231808202566867e-09,
)

TERM_MAX = 32000.0
TINY = 1e-30


def scaled_cos(angle):
    turns = jnp.round(angle * jnp.float32(TURN))
    rest = (angle - turns * jnp.float32(TURN_HI)) - turns * jnp.float32(TURN_LO)
    square = rest * rest
    value = jnp.float32(COS[-1] * SCALE)
    for c in COS[-2::-1]:
        value = value * square + jnp.float32(c * SCALE)
    return value


def rounded_copies(direction_ref, copies_ref):
    rounded = direction_ref[...].astype(copies_ref.dtype)
    copies_ref[...] = jnp.broadcast_to(rounded[None], copies_ref.shape)


def exchange(blocks, axes):
    return lax.all_to_all(blocks, axes, 0, 0, axis_index_groups=[ORDERS[axes]], tiled=True)


def spread(value, axes):
    n = lax.axis_size(axes)
    copies = jnp.broadcast_to(value[None], (n,) + value.shape)
    return exchange(copies, axes)


def total_of(row, axes):
    return jnp.sum(spread(row, axes), axis=0)


def listed(cols, own):
    cols = jnp.roll(cols, -2, axis=1)
    return jnp.roll(cols, -4 * own, axis=2).reshape(cols.shape[0], -1)


def body(descriptors, freqs, phases, row_weight, resid, coef, direction, ridge, gamma):
    rows_dev, desc = descriptors.shape
    targets = resid.shape[1]
    own = direction.shape[0]
    zl = lax.axis_index("zl")
    swap = [(0, 1), (1, 0)]
    n_plane, n_column = lax.axis_size(PLANE), lax.axis_size(COLUMN)

    def both(mine, peer):
        return jnp.where(zl == 0, jnp.concatenate([mine, peer]), jnp.concatenate([peer, mine]))

    copies = pl.pallas_call(
        rounded_copies,
        out_shape=jax.ShapeDtypeStruct((n_plane, own, targets), jnp.bfloat16),
        cost_estimate=pl.CostEstimate(flops=0, transcendentals=0, bytes_accessed=4 * own * targets + 2 * n_plane * own * targets),
    )(direction)
    copies, descriptors, resid, row_weight, freqs, phases, direction = lax.optimization_barrier(
        (copies, descriptors, resid, row_weight, freqs, phases, direction)
    )
    gathered = exchange(copies, PLANE).reshape(-1, targets)

    rows_x = both(descriptors, lax.ppermute(descriptors, "zl", swap))
    packed = jnp.concatenate([resid, row_weight.reshape(-1, targets)])
    peer = lax.ppermute(packed, "zl", swap)
    rows_resid = both(resid, peer[:rows_dev])
    rows_weight = both(row_weight, peer[rows_dev:].reshape(-1))

    n_x = lax.axis_size("x")
    freq_cols = freqs.reshape(desc, n_x, 2, -1)
    freq_cols = listed(lax.dynamic_index_in_dim(freq_cols, zl, 2, keepdims=False), own)
    phase_cols = lax.dynamic_index_in_dim(phases.reshape(n_x, 2, -1), zl, 1, keepdims=False)
    phase_cols = listed(phase_cols[None], own)[0]
    angle = jnp.dot(rows_x, freq_cols, preferred_element_type=jnp.float32) + phase_cols[None, :]
    feats = scaled_cos(angle).astype(jnp.bfloat16)
    penalty = ridge * jnp.sum(direction * direction, axis=0)
    extra = jnp.broadcast_to(penalty[None, None], (n_column, 8, targets))
    rows_weight = jnp.broadcast_to(rows_weight[:, None], (2 * rows_dev, targets))
    resid_size = jnp.sum(jnp.abs(rows_weight * rows_resid), axis=0)
    kind = lax.broadcasted_iota(jnp.int32, (4, targets), 0)
    gathered, feats, rows_resid, rows_weight, extra, resid_size, lower, kind = lax.optimization_barrier(
        (gathered, feats, rows_resid, rows_weight, extra, resid_size, zl == 0, kind)
    )
    partial = jnp.dot(feats, gathered, preferred_element_type=jnp.float32)

    sent = jnp.concatenate([partial.reshape(n_column, -1, targets), extra], axis=1)
    came = jnp.sum(exchange(sent, COLUMN), axis=0)
    share = came.shape[0] - 8
    image = rows_weight * spread(came[:share], COLUMN).reshape(-1, targets)
    local = jnp.where(kind == 0, (jnp.sum(image * image, axis=0) + came[share])[None], resid_size[None])
    local = jnp.where(kind == 2, jnp.sum(jnp.abs(rows_weight * image), axis=0)[None], local)
    seen = spread(local, PLANE)
    alpha = gamma / jnp.sum(seen[:, 0], axis=0)
    bound = jnp.max(seen[:, 1], axis=0) + jnp.abs(alpha) * jnp.max(seen[:, 2], axis=0)
    scale = TERM_MAX / jnp.maximum(SCALE * bound, TINY)
    coef_new = coef + alpha[None, :] * direction
    rows_new = rows_resid - alpha[None, :] * image
    resid_new = lax.optimization_barrier(jnp.where(lower, rows_new[:rows_dev], rows_new[rows_dev:]))
    peer_new = jnp.where(lower, rows_new[rows_dev:], rows_new[:rows_dev])
    rows_new = jnp.where(lower, jnp.concatenate([resid_new, peer_new]), jnp.concatenate([peer_new, resid_new]))
    weighted_b = (rows_weight * rows_new).astype(jnp.bfloat16)
    weighted_b, coef_new, resid_new = lax.optimization_barrier((weighted_b, coef_new, resid_new))

    terms = lax.dot_general(
        feats, weighted_b, (((0,), (0,)), ((), ())), preferred_element_type=jnp.float32
    )
    terms = (terms * scale[None, :]).astype(jnp.float16)
    terms = exchange(terms.reshape(n_plane, own, targets), PLANE)
    summed = jnp.sum(terms.astype(jnp.float32), axis=0) * (1.0 / scale)[None, :]
    gradient = summed - ridge[None, :] * coef_new
    gamma_new = total_of(total_of(jnp.sum(gradient * gradient, axis=0)[None], PLANE), COLUMN)[0]
    direction_new = gradient + (gamma_new / gamma)[None, :] * direction
    return (coef_new, resid_new, direction_new, gamma_new)


def solution(mesh):
    cut = Mesh(mesh.devices.reshape(SIZES), AXES)
    split = P(FEAT + ROWS, None)
    return jax.shard_map(
        body,
        mesh=cut,
        in_specs=(P(ROWS, None), P(None, FEAT), P(FEAT), P(ROWS), P(ROWS, None), split, split, P(), P()),
        out_specs=(split, P(ROWS, None), split, P()),
        check_vma=False,
    )
```

```python
import jax
import jax.numpy as jnp
import numpy as np
from jax import lax
from jax.experimental import pallas as pl
from jax.sharding import Mesh, PartitionSpec as P

AXES = ("x", "zl", "y", "zh", "core")
SIZES = (4, 2, 8, 4, 2)
ROWS = ("x", "zl", "y")
FEAT = ("zh", "core")
PLANE = ("x", "y")
COLUMN = ("zl", "zh", "core")
LATE_ZL, LATE_ZH = 1, 2

PLANE_ORDER = [((x + 2) % 4) * 8 + (y + 4) % 8 for x in range(4) for y in range(8)]
COLUMN_ORDER = [((i // 8 + LATE_ZL) % 2) * 8 + ((i // 2 + LATE_ZH) % 4) * 2 + i % 2 for i in range(16)]
ORDERS = {PLANE: PLANE_ORDER, COLUMN: COLUMN_ORDER}

SCALE = 2.0**-7
TURN = 1.0 / (2.0 * np.pi)
COS = (
    1.0,
    -0.49999988079071045,
    0.041666485369205475,
    -0.0013887786772102118,
    2.476951885910239e-05,
    -2.707541852942086e-07,
    1.7231808202566867e-09,
)

TURN_COS = [c * SCALE * (2.0 * np.pi) ** (2 * i) for i, c in enumerate(COS)]
TERM_MAX = 32000.0
TINY = 1e-30


def scaled_cos(angle):
    turns = angle * jnp.float32(TURN)
    rest = turns - jnp.round(turns)
    square = rest * rest
    value = jnp.float32(TURN_COS[-1])
    for c in TURN_COS[-2::-1]:
        value = value * square + jnp.float32(c)
    return value


def rounded_copies(direction_ref, copies_ref):
    rounded = direction_ref[...].astype(copies_ref.dtype)
    copies_ref[...] = jnp.broadcast_to(rounded[None], copies_ref.shape)


def exchange(blocks, axes):
    return lax.all_to_all(blocks, axes, 0, 0, axis_index_groups=[ORDERS[axes]], tiled=True)


def spread(value, axes):
    n = lax.axis_size(axes)
    copies = jnp.broadcast_to(value[None], (n,) + value.shape)
    return exchange(copies, axes)


def total_of(row, axes):
    return jnp.sum(spread(row, axes), axis=0)


def listed(cols, own):
    cols = jnp.roll(cols, -2, axis=1)
    return jnp.roll(cols, -4 * own, axis=2).reshape(cols.shape[0], -1)


def body(descriptors, freqs, phases, row_weight, resid, coef, direction, ridge, gamma):
    rows_dev, desc = descriptors.shape
    targets = resid.shape[1]
    own = direction.shape[0]
    zl = lax.axis_index("zl")
    swap = [(0, 1), (1, 0)]
    n_plane, n_column = lax.axis_size(PLANE), lax.axis_size(COLUMN)

    def both(mine, peer):
        return jnp.where(zl == 0, jnp.concatenate([mine, peer]), jnp.concatenate([peer, mine]))

    copies = pl.pallas_call(
        rounded_copies,
        out_shape=jax.ShapeDtypeStruct((n_plane, own, targets), jnp.bfloat16),
        cost_estimate=pl.CostEstimate(flops=0, transcendentals=0, bytes_accessed=4 * own * targets + 2 * n_plane * own * targets),
    )(direction)
    copies, descriptors, resid, row_weight, freqs, phases, direction = lax.optimization_barrier(
        (copies, descriptors, resid, row_weight, freqs, phases, direction)
    )
    gathered = exchange(copies, PLANE).reshape(-1, targets)

    rows_x = both(descriptors, lax.ppermute(descriptors, "zl", swap))
    packed = jnp.concatenate([resid, row_weight.reshape(-1, targets)])
    peer = lax.ppermute(packed, "zl", swap)
    rows_resid = both(resid, peer[:rows_dev])
    rows_weight = both(row_weight, peer[rows_dev:].reshape(-1))

    n_x = lax.axis_size("x")
    freq_cols = freqs.reshape(desc, n_x, 2, -1)
    freq_cols = listed(lax.dynamic_index_in_dim(freq_cols, zl, 2, keepdims=False), own)
    phase_cols = lax.dynamic_index_in_dim(phases.reshape(n_x, 2, -1), zl, 1, keepdims=False)
    phase_cols = listed(phase_cols[None], own)[0]
    angle = jnp.dot(rows_x, freq_cols, preferred_element_type=jnp.float32) + phase_cols[None, :]
    feats = scaled_cos(angle).astype(jnp.bfloat16)
    penalty = ridge * jnp.sum(direction * direction, axis=0)
    extra = jnp.broadcast_to(penalty[None, None], (n_column, 8, targets))
    rows_weight = jnp.broadcast_to(rows_weight[:, None], (2 * rows_dev, targets))
    resid_size = jnp.sum(jnp.abs(rows_weight * rows_resid), axis=0)
    kind = lax.broadcasted_iota(jnp.int32, (4, targets), 0)
    gathered, feats, rows_resid, rows_weight, extra, resid_size, lower, kind = lax.optimization_barrier(
        (gathered, feats, rows_resid, rows_weight, extra, resid_size, zl == 0, kind)
    )
    partial = jnp.dot(feats, gathered, preferred_element_type=jnp.float32)

    sent = jnp.concatenate([partial.reshape(n_column, -1, targets), extra], axis=1)
    came = jnp.sum(exchange(sent, COLUMN), axis=0)
    share = came.shape[0] - 8
    image = rows_weight * spread(came[:share], COLUMN).reshape(-1, targets)
    local = jnp.where(kind == 0, (jnp.sum(image * image, axis=0) + came[share])[None], resid_size[None])
    local = jnp.where(kind == 2, jnp.sum(jnp.abs(rows_weight * image), axis=0)[None], local)
    seen = spread(local, PLANE)
    alpha = gamma / jnp.sum(seen[:, 0], axis=0)
    bound = jnp.max(seen[:, 1], axis=0) + jnp.abs(alpha) * jnp.max(seen[:, 2], axis=0)
    scale = TERM_MAX / jnp.maximum(SCALE * bound, TINY)
    coef_new = coef + alpha[None, :] * direction
    rows_new = rows_resid - alpha[None, :] * image
    resid_new = lax.optimization_barrier(jnp.where(lower, rows_new[:rows_dev], rows_new[rows_dev:]))
    peer_new = jnp.where(lower, rows_new[rows_dev:], rows_new[:rows_dev])
    rows_new = jnp.where(lower, jnp.concatenate([resid_new, peer_new]), jnp.concatenate([peer_new, resid_new]))
    weighted_b = (rows_weight * rows_new).astype(jnp.bfloat16)
    weighted_b, coef_new, resid_new = lax.optimization_barrier((weighted_b, coef_new, resid_new))

    terms = lax.dot_general(
        feats, weighted_b, (((0,), (0,)), ((), ())), preferred_element_type=jnp.float32
    )
    terms = (terms * scale[None, :]).astype(jnp.float16)
    terms = exchange(terms.reshape(n_plane, own, targets), PLANE)
    summed = jnp.sum(terms.astype(jnp.float32), axis=0) * (1.0 / scale)[None, :]
    gradient = summed - ridge[None, :] * coef_new
    gamma_new = total_of(total_of(jnp.sum(gradient * gradient, axis=0)[None], COLUMN), PLANE)[0]
    direction_new = gradient + (gamma_new / gamma)[None, :] * direction
    return (coef_new, resid_new, direction_new, gamma_new)


def solution(mesh):
    cut = Mesh(mesh.devices.reshape(SIZES), AXES)
    split = P(FEAT + ROWS, None)
    return jax.shard_map(
        body,
        mesh=cut,
        in_specs=(P(ROWS, None), P(None, FEAT), P(FEAT), P(ROWS), P(ROWS, None), split, split, P(), P()),
        out_specs=(split, P(ROWS, None), split, P()),
        check_vma=False,
    )
```

```python
import jax
import jax.numpy as jnp
import numpy as np
from jax import lax
from jax.experimental import pallas as pl
from jax.sharding import Mesh, PartitionSpec as P

AXES = ("x", "zl", "y", "zh", "core")
SIZES = (4, 2, 8, 4, 2)
ROWS = ("x", "zl", "y")
FEAT = ("zh", "core")
PLANE = ("x", "y")
COLUMN = ("zl", "zh", "core")
LATE_ZL, LATE_ZH = 0, 3

PLANE_ORDER = [((x + 2) % 4) * 8 + (y + 4) % 8 for x in range(4) for y in range(8)]
COLUMN_ORDER = [((i // 8 + LATE_ZL) % 2) * 8 + ((i // 2 + LATE_ZH) % 4) * 2 + i % 2 for i in range(16)]
ORDERS = {PLANE: PLANE_ORDER, COLUMN: COLUMN_ORDER}

SCALE = 2.0**-7
TURN = 1.0 / (2.0 * np.pi)
TURN_HI = 6.28125
TURN_LO = 2.0 * np.pi - 6.28125
COS = (
    1.0,
    -0.49999988079071045,
    0.041666485369205475,
    -0.0013887786772102118,
    2.476951885910239e-05,
    -2.707541852942086e-07,
    1.7231808202566867e-09,
)

TERM_MAX = 32000.0
TINY = 1e-30


def scaled_cos(angle):
    turns = jnp.round(angle * jnp.float32(TURN))
    rest = (angle - turns * jnp.float32(TURN_HI)) - turns * jnp.float32(TURN_LO)
    square = rest * rest
    value = jnp.float32(COS[-1] * SCALE)
    for c in COS[-2::-1]:
        value = value * square + jnp.float32(c * SCALE)
    return value


def rounded_copies(direction_ref, copies_ref):
    rounded = direction_ref[...].astype(copies_ref.dtype)
    copies_ref[...] = jnp.broadcast_to(rounded[None], copies_ref.shape)


def exchange(blocks, axes):
    return lax.all_to_all(blocks, axes, 0, 0, axis_index_groups=[ORDERS[axes]], tiled=True)


def spread(value, axes):
    n = lax.axis_size(axes)
    copies = jnp.broadcast_to(value[None], (n,) + value.shape)
    return exchange(copies, axes)


def total_of(row, axes):
    return jnp.sum(spread(row, axes), axis=0)


def listed(cols, own):
    cols = jnp.roll(cols, -2, axis=1)
    return jnp.roll(cols, -4 * own, axis=2).reshape(cols.shape[0], -1)


def body(descriptors, freqs, phases, row_weight, resid, coef, direction, ridge, gamma):
    rows_dev, desc = descriptors.shape
    targets = resid.shape[1]
    own = direction.shape[0]
    zl = lax.axis_index("zl")
    swap = [(0, 1), (1, 0)]
    n_plane, n_column = lax.axis_size(PLANE), lax.axis_size(COLUMN)

    def both(mine, peer):
        return jnp.where(zl == 0, jnp.concatenate([mine, peer]), jnp.concatenate([peer, mine]))

    copies = pl.pallas_call(
        rounded_copies,
        out_shape=jax.ShapeDtypeStruct((n_plane, own, targets), jnp.bfloat16),
        cost_estimate=pl.CostEstimate(flops=0, transcendentals=0, bytes_accessed=4 * own * targets + 2 * n_plane * own * targets),
    )(direction)
    copies, descriptors, resid, row_weight, freqs, phases, direction = lax.optimization_barrier(
        (copies, descriptors, resid, row_weight, freqs, phases, direction)
    )
    gathered = exchange(copies, PLANE).reshape(-1, targets)

    rows_x = both(descriptors, lax.ppermute(descriptors, "zl", swap))
    packed = jnp.concatenate([resid, row_weight.reshape(-1, targets)])
    peer = lax.ppermute(packed, "zl", swap)
    rows_resid = both(resid, peer[:rows_dev])
    rows_weight = both(row_weight, peer[rows_dev:].reshape(-1))

    n_x = lax.axis_size("x")
    freq_cols = freqs.reshape(desc, n_x, 2, -1)
    freq_cols = listed(lax.dynamic_index_in_dim(freq_cols, zl, 2, keepdims=False), own)
    phase_cols = lax.dynamic_index_in_dim(phases.reshape(n_x, 2, -1), zl, 1, keepdims=False)
    phase_cols = listed(phase_cols[None], own)[0]
    angle = jnp.dot(rows_x, freq_cols, preferred_element_type=jnp.float32) + phase_cols[None, :]
    feats = scaled_cos(angle).astype(jnp.bfloat16)
    penalty = ridge * jnp.sum(direction * direction, axis=0)
    extra = jnp.broadcast_to(penalty[None, None], (n_column, 8, targets))
    rows_weight = jnp.broadcast_to(rows_weight[:, None], (2 * rows_dev, targets))
    resid_size = jnp.sum(jnp.abs(rows_weight * rows_resid), axis=0)
    kind = lax.broadcasted_iota(jnp.int32, (4, targets), 0)
    gathered, feats, rows_resid, rows_weight, extra, resid_size, lower, kind = lax.optimization_barrier(
        (gathered, feats, rows_resid, rows_weight, extra, resid_size, zl == 0, kind)
    )
    partial = jnp.dot(feats, gathered, preferred_element_type=jnp.float32)

    sent = jnp.concatenate([partial.reshape(n_column, -1, targets), extra], axis=1)
    came = jnp.sum(exchange(sent, COLUMN), axis=0)
    share = came.shape[0] - 8
    image = rows_weight * spread(came[:share], COLUMN).reshape(-1, targets)
    local = jnp.where(kind == 0, (jnp.sum(image * image, axis=0) + came[share])[None], resid_size[None])
    local = jnp.where(kind == 2, jnp.sum(jnp.abs(rows_weight * image), axis=0)[None], local)
    seen = spread(local, PLANE)
    alpha = gamma / jnp.sum(seen[:, 0], axis=0)
    bound = jnp.max(seen[:, 1], axis=0) + jnp.abs(alpha) * jnp.max(seen[:, 2], axis=0)
    scale = TERM_MAX / jnp.maximum(SCALE * bound, TINY)
    coef_new = coef + alpha[None, :] * direction
    rows_new = rows_resid - alpha[None, :] * image
    resid_new = lax.optimization_barrier(jnp.where(lower, rows_new[:rows_dev], rows_new[rows_dev:]))
    peer_new = jnp.where(lower, rows_new[rows_dev:], rows_new[:rows_dev])
    rows_new = jnp.where(lower, jnp.concatenate([resid_new, peer_new]), jnp.concatenate([peer_new, resid_new]))
    weighted_b = (rows_weight * rows_new).astype(jnp.bfloat16)
    weighted_b, coef_new, resid_new = lax.optimization_barrier((weighted_b, coef_new, resid_new))

    terms = lax.dot_general(
        feats, weighted_b, (((0,), (0,)), ((), ())), preferred_element_type=jnp.float32
    )
    terms = (terms * scale[None, :]).astype(jnp.float16)
    terms = exchange(terms.reshape(n_plane, own, targets), PLANE)
    summed = jnp.sum(terms.astype(jnp.float32), axis=0) * (1.0 / scale)[None, :]
    gradient = summed - ridge[None, :] * coef_new
    gamma_new = total_of(total_of(jnp.sum(gradient * gradient, axis=0)[None], COLUMN), PLANE)[0]
    direction_new = gradient + (gamma_new / gamma)[None, :] * direction
    return (coef_new, resid_new, direction_new, gamma_new)


def solution(mesh):
    cut = Mesh(mesh.devices.reshape(SIZES), AXES)
    split = P(FEAT + ROWS, None)
    return jax.shard_map(
        body,
        mesh=cut,
        in_specs=(P(ROWS, None), P(None, FEAT), P(FEAT), P(ROWS), P(ROWS, None), split, split, P(), P()),
        out_specs=(split, P(ROWS, None), split, P()),
        check_vma=False,
    )
```

```python
import jax
import jax.numpy as jnp
import numpy as np
from jax import lax
from jax.experimental import pallas as pl
from jax.sharding import Mesh, PartitionSpec as P

AXES = ("x", "zl", "y", "zh", "core")
SIZES = (4, 2, 8, 4, 2)
ROWS = ("x", "zl", "y")
FEAT = ("zh", "core")
PLANE = ("x", "y")
COLUMN = ("zl", "zh", "core")
LATE_ZL, LATE_ZH = 1, 2

PLANE_ORDER = [((x + 1) % 4) * 8 + (y + 4) % 8 for x in range(4) for y in range(8)]
COLUMN_ORDER = [((i // 8 + LATE_ZL) % 2) * 8 + ((i // 2 + LATE_ZH) % 4) * 2 + i % 2 for i in range(16)]
ORDERS = {PLANE: PLANE_ORDER, COLUMN: COLUMN_ORDER}

SCALE = 2.0**-7
TURN = 1.0 / (2.0 * np.pi)
TURN_HI = 6.28125
TURN_LO = 2.0 * np.pi - 6.28125
COS = (
    1.0,
    -0.49999988079071045,
    0.041666485369205475,
    -0.0013887786772102118,
    2.476951885910239e-05,
    -2.707541852942086e-07,
    1.7231808202566867e-09,
)

TERM_MAX = 32000.0
TINY = 1e-30


def scaled_cos(angle):
    turns = jnp.round(angle * jnp.float32(TURN))
    rest = (angle - turns * jnp.float32(TURN_HI)) - turns * jnp.float32(TURN_LO)
    square = rest * rest
    value = jnp.float32(COS[-1] * SCALE)
    for c in COS[-2::-1]:
        value = value * square + jnp.float32(c * SCALE)
    return value


def rounded_copies(direction_ref, copies_ref):
    rounded = direction_ref[...].astype(copies_ref.dtype)
    copies_ref[...] = jnp.broadcast_to(rounded[None], copies_ref.shape)


def exchange(blocks, axes):
    return lax.all_to_all(blocks, axes, 0, 0, axis_index_groups=[ORDERS[axes]], tiled=True)


def spread(value, axes):
    n = lax.axis_size(axes)
    copies = jnp.broadcast_to(value[None], (n,) + value.shape)
    return exchange(copies, axes)


def total_of(row, axes):
    return jnp.sum(spread(row, axes), axis=0)


def listed(cols, own):
    cols = jnp.roll(cols, -1, axis=1)
    return jnp.roll(cols, -4 * own, axis=2).reshape(cols.shape[0], -1)


def body(descriptors, freqs, phases, row_weight, resid, coef, direction, ridge, gamma):
    rows_dev, desc = descriptors.shape
    targets = resid.shape[1]
    own = direction.shape[0]
    zl = lax.axis_index("zl")
    swap = [(0, 1), (1, 0)]
    n_plane, n_column = lax.axis_size(PLANE), lax.axis_size(COLUMN)

    def both(mine, peer):
        return jnp.where(zl == 0, jnp.concatenate([mine, peer]), jnp.concatenate([peer, mine]))

    copies = pl.pallas_call(
        rounded_copies,
        out_shape=jax.ShapeDtypeStruct((n_plane, own, targets), jnp.bfloat16),
        cost_estimate=pl.CostEstimate(flops=0, transcendentals=0, bytes_accessed=4 * own * targets + 2 * n_plane * own * targets),
    )(direction)
    copies, descriptors, resid, row_weight, freqs, phases, direction = lax.optimization_barrier(
        (copies, descriptors, resid, row_weight, freqs, phases, direction)
    )
    gathered = exchange(copies, PLANE).reshape(-1, targets)

    rows_x = both(descriptors, lax.ppermute(descriptors, "zl", swap))
    packed = jnp.concatenate([resid, row_weight.reshape(-1, targets)])
    peer = lax.ppermute(packed, "zl", swap)
    rows_resid = both(resid, peer[:rows_dev])
    rows_weight = both(row_weight, peer[rows_dev:].reshape(-1))

    n_x = lax.axis_size("x")
    freq_cols = freqs.reshape(desc, n_x, 2, -1)
    freq_cols = listed(lax.dynamic_index_in_dim(freq_cols, zl, 2, keepdims=False), own)
    phase_cols = lax.dynamic_index_in_dim(phases.reshape(n_x, 2, -1), zl, 1, keepdims=False)
    phase_cols = listed(phase_cols[None], own)[0]
    angle = jnp.dot(rows_x, freq_cols, preferred_element_type=jnp.float32) + phase_cols[None, :]
    feats = scaled_cos(angle).astype(jnp.bfloat16)
    penalty = ridge * jnp.sum(direction * direction, axis=0)
    extra = jnp.broadcast_to(penalty[None, None], (n_column, 8, targets))
    rows_weight = jnp.broadcast_to(rows_weight[:, None], (2 * rows_dev, targets))
    resid_size = jnp.sum(jnp.abs(rows_weight * rows_resid), axis=0)
    kind = lax.broadcasted_iota(jnp.int32, (4, targets), 0)
    gathered, feats, rows_resid, rows_weight, extra, resid_size, lower, kind = lax.optimization_barrier(
        (gathered, feats, rows_resid, rows_weight, extra, resid_size, zl == 0, kind)
    )
    partial = jnp.dot(feats, gathered, preferred_element_type=jnp.float32)

    sent = jnp.concatenate([partial.reshape(n_column, -1, targets), extra], axis=1)
    came = jnp.sum(exchange(sent, COLUMN), axis=0)
    share = came.shape[0] - 8
    image = rows_weight * spread(came[:share], COLUMN).reshape(-1, targets)
    local = jnp.where(kind == 0, (jnp.sum(image * image, axis=0) + came[share])[None], resid_size[None])
    local = jnp.where(kind == 2, jnp.sum(jnp.abs(rows_weight * image), axis=0)[None], local)
    seen = spread(local, PLANE)
    alpha = gamma / jnp.sum(seen[:, 0], axis=0)
    bound = jnp.max(seen[:, 1], axis=0) + jnp.abs(alpha) * jnp.max(seen[:, 2], axis=0)
    scale = TERM_MAX / jnp.maximum(SCALE * bound, TINY)
    coef_new = coef + alpha[None, :] * direction
    rows_new = rows_resid - alpha[None, :] * image
    resid_new = lax.optimization_barrier(jnp.where(lower, rows_new[:rows_dev], rows_new[rows_dev:]))
    peer_new = jnp.where(lower, rows_new[rows_dev:], rows_new[:rows_dev])
    rows_new = jnp.where(lower, jnp.concatenate([resid_new, peer_new]), jnp.concatenate([peer_new, resid_new]))
    weighted_b = (rows_weight * rows_new).astype(jnp.bfloat16)
    weighted_b, coef_new, resid_new = lax.optimization_barrier((weighted_b, coef_new, resid_new))

    terms = lax.dot_general(
        feats, weighted_b, (((0,), (0,)), ((), ())), preferred_element_type=jnp.float32
    )
    terms = (terms * scale[None, :]).astype(jnp.float16)
    terms = exchange(terms.reshape(n_plane, own, targets), PLANE)
    summed = jnp.sum(terms.astype(jnp.float32), axis=0) * (1.0 / scale)[None, :]
    gradient = summed - ridge[None, :] * coef_new
    gamma_new = total_of(total_of(jnp.sum(gradient * gradient, axis=0)[None], COLUMN), PLANE)[0]
    direction_new = gradient + (gamma_new / gamma)[None, :] * direction
    return (coef_new, resid_new, direction_new, gamma_new)


def solution(mesh):
    cut = Mesh(mesh.devices.reshape(SIZES), AXES)
    split = P(FEAT + ROWS, None)
    return jax.shard_map(
        body,
        mesh=cut,
        in_specs=(P(ROWS, None), P(None, FEAT), P(FEAT), P(ROWS), P(ROWS, None), split, split, P(), P()),
        out_specs=(split, P(ROWS, None), split, P()),
        check_vma=False,
    )
```
